256 devices in a mesh: dp: 32 (over y_hi, z, core), fsdp: 8 (over x, y_lo).
Axes of the slice: x: 4, y: 4 (y_hi: 2, y_lo: 2; y = y_hi * 2 + y_lo), z: 8, core: 2. Of those that a mesh axis runs over, the one named last changes fastest.
Arguments:
- tokens: bfloat16 [4096, 4096], P(('fsdp', 'dp')), may hold values from -6 to 6
- upstream: bfloat16 [4096, 4096], P(('fsdp', 'dp')), may hold values from -0.375 to 0.375
- old_master: float32 [4096, 3, 5632], P(('fsdp', 'dp')), may hold values from -0.09375 to 0.09375
- old_first: float32 [4096, 3, 5632], P(('fsdp', 'dp')), may hold values from -3 to 3
- old_second: float32 [4096, 3, 5632], P(('fsdp', 'dp')), may hold values from 0.01 to 4
- grown_master: float32 [4096, 3, 2560], P(('fsdp', 'dp')), may hold values from -0.09375 to 0.09375
- grown_first: float32 [4096, 3, 2560], P(('fsdp', 'dp')), may hold values from -3 to 3
- grown_second: float32 [4096, 3, 2560], P(('fsdp', 'dp')), may hold values from 0.01 to 4
- grow_mask: float32 [2560], replicated, may hold values from 0.1 to 1
Outputs:
- layer_output: bfloat16 [4096, 4096], P(('fsdp', 'dp'))
- new_master: float32 [4096, 3, 8192], P('fsdp', None, 'dp')
- new_first: float32 [4096, 3, 8192], P('fsdp', None, 'dp')
- new_second: float32 [4096, 3, 8192], P('fsdp', None, 'dp')
The draws below stay inside these ranges and needn't reach their ends.
All inputs are finite; a program needn't handle non-finite values.
Results may differ from the reference program's by a relative error of at most 0.019.
Values may be sent and summed in bfloat16 or wider, within the bound.
A program may use at most 128 MiB of HBM per device.

```python
import math
import jax
import jax.numpy as jnp
from jax import lax

D = 4096
FF_OLD = 5632
FF_NEW = 8192
STEP = 1000
FF_GROW = 2560
TOKENS = 4096
N_DP = 32
N_FSDP = 8


def shard_levels(key, shape, cuts, smallest, high):
    level = 1.0
    for dim, shards_of in cuts:
        draws = jax.random.uniform(jax.random.fold_in(jax.random.fold_in(key, 6), dim), (shards_of,), jnp.float32, smallest / len(cuts), high / len(cuts))
        level = level * jnp.repeat(jnp.exp(draws), shape[dim] // shards_of).reshape((-1,) + (1,) * (len(shape) - 1 - dim))
    return level


def noise(key, extent, deviation, most, cuts=(), held_as=jnp.bfloat16):
    entries = jax.random.normal(key, extent, jnp.float32) * deviation
    if len(cuts) > 0:
        entries = shard_levels(key, extent, cuts, -0.22, 0.18) * entries
    return jnp.clip(entries, min=-most, max=most).astype(held_as)


def setup_inputs(seed: int = 0) -> dict:
    splits = jax.random.split(jax.random.key(seed), 10)
    return {
        "tokens": noise(splits[0], (TOKENS, D), 1.0, 6.0, ((0, 256),)),
        "upstream": noise(splits[1], (TOKENS, D), 0.0625, 0.375, ((0, 256),)),
        "old_master": noise(splits[2], (D, 3, FF_OLD), D ** -0.5, 0.09375, ((0, 256),), jnp.float32),
        "old_first": noise(splits[3], (D, 3, FF_OLD), 0.5, 3.0, ((0, 256),), jnp.float32),
        "old_second": jnp.clip(jnp.exp(math.log(4.0) - 5.9914646 * jax.random.uniform(splits[4], (D, 3, FF_OLD), jnp.float32) ** shard_levels(splits[4], (D, 3, FF_OLD), ((0, 256),), -0.2, 0.2)), 0.01, 4.0),
        "grown_master": noise(splits[5], (D, 3, FF_GROW), D ** -0.5, 0.09375, ((0, 256),), jnp.float32),
        "grown_first": noise(splits[6], (D, 3, FF_GROW), 0.5, 3.0, ((0, 256),), jnp.float32),
        "grown_second": jnp.clip(jnp.exp(math.log(4.0) - 5.9914646 * jax.random.uniform(splits[7], (D, 3, FF_GROW), jnp.float32) ** shard_levels(splits[7], (D, 3, FF_GROW), ((0, 256),), -0.2, 0.2)), 0.01, 4.0),
        "grow_mask": jnp.clip(jax.random.uniform(splits[8], (FF_GROW,), jnp.float32, 0.1, 1.0), 0.1, 1.0),
    }


beta_first = 0.9
beta_second = 0.999
adam_epsilon = 1e-08
learn_rate = 0.001
weight_decay = 0.1

def contract_rows(left_part, right_part):
    left_part = left_part.astype(jnp.float32)
    right_part = right_part.astype(jnp.float32)
    return lax.dot_general(left_part, right_part, (((0,), (0,)), ((), ())), preferred_element_type=jnp.float32)

def contract_last(left_part, right_part):
    left_part = left_part.astype(jnp.float32)
    right_part = right_part.astype(jnp.float32)
    return lax.dot_general(left_part, right_part, (((1,), (1,)), ((), ())), preferred_element_type=jnp.float32)

def adam_update(master, first_moment, second_moment, gradients):
    new_first = beta_first * first_moment + (1.0 - beta_first) * gradients
    new_second = beta_second * second_moment + (1.0 - beta_second) * gradients * gradients
    first_hat = new_first / (1.0 - beta_first ** STEP)
    second_hat = new_second / (1.0 - beta_second ** STEP)
    new_master = master - learn_rate * (first_hat / (jnp.sqrt(second_hat) + adam_epsilon) + weight_decay * master)
    return (new_master, new_first, new_second)

def reference(tokens, upstream, old_master, old_first, old_second, grown_master, grown_first, grown_second, grow_mask):
    master = jnp.concatenate([old_master, grown_master], axis=2)
    first_moment = jnp.concatenate([old_first, grown_first], axis=2)
    second_moment = jnp.concatenate([old_second, grown_second], axis=2)
    weights = master.astype(jnp.bfloat16)
    scales = jnp.concatenate([jnp.ones((FF_OLD,), jnp.float32), grow_mask])
    gate_value = jnp.dot(tokens, weights[:, 0, :], preferred_element_type=jnp.float32)
    up_value = jnp.dot(tokens, weights[:, 1, :], preferred_element_type=jnp.float32)
    sigmoid_gate = jax.nn.sigmoid(gate_value)
    activated = gate_value * sigmoid_gate
    hidden = (activated * up_value * scales).astype(jnp.bfloat16)
    down_weights = weights[:, 2, :]
    block_width = FF_NEW // N_DP
    hidden_blocks = hidden.reshape(TOKENS, N_DP, block_width).transpose(1, 0, 2)
    down_blocks = down_weights.reshape(D, N_DP, block_width).transpose(1, 0, 2)

    def add_block(running, pieces):
        part_sum = contract_last(pieces[0], pieces[1])
        rounded = lax.optimization_barrier(part_sum.astype(jnp.bfloat16))
        return (running + rounded.astype(jnp.float32), None)
    summed, unused = lax.scan(add_block, jnp.zeros((TOKENS, D), jnp.float32), (hidden_blocks, down_blocks))
    layer_output = summed.astype(jnp.bfloat16)
    back_hidden = jnp.dot(upstream, down_weights, preferred_element_type=jnp.float32) * scales
    gate_back = (back_hidden * up_value * sigmoid_gate * (1.0 + gate_value * (1.0 - sigmoid_gate))).astype(jnp.bfloat16)
    up_back = (back_hidden * activated).astype(jnp.bfloat16)
    group_rows = TOKENS // N_FSDP

    def grouped(array):
        return array.reshape(N_FSDP, group_rows, array.shape[1])

    def add_group(running, pieces):
        rows_in, rows_back, gate_part, up_part, hidden_part = pieces
        stacked = jnp.stack([contract_rows(rows_in, gate_part), contract_rows(rows_in, up_part), contract_rows(rows_back, hidden_part)], axis=1)
        rounded = lax.optimization_barrier(stacked.astype(jnp.bfloat16))
        return (running + rounded.astype(jnp.float32), None)
    gradients, unused_too = lax.scan(add_group, jnp.zeros((D, 3, FF_NEW), jnp.float32), (grouped(tokens), grouped(upstream), grouped(gate_back), grouped(up_back), grouped(hidden)))
    new_master, new_first, new_second = adam_update(master, first_moment, second_moment, gradients)
    return (layer_output, new_master, new_first, new_second)
```

```python
import functools

import jax
import jax.numpy as jnp
from jax import lax
from jax.experimental import pallas as pl
from jax.experimental.pallas import tpu as pltpu
from jax.sharding import PartitionSpec as P

STEP = 1000

beta_first = 0.9
beta_second = 0.999
adam_epsilon = 1e-08
learn_rate = 0.001
weight_decay = 0.1

BF = jnp.bfloat16
F32 = jnp.float32
MESH = pl.DeviceIdType.MESH

NX, NZ, NDP = 4, 8, 32
PLACE = {k: i for i, k in enumerate((0, 1, 7, 2, 6, 3, 5, 4))}


def adam_update(master, first_moment, second_moment, gradients):
    new_first = beta_first * first_moment + (1.0 - beta_first) * gradients
    new_second = beta_second * second_moment + (1.0 - beta_second) * gradients * gradients
    first_hat = new_first / (1.0 - beta_first**STEP)
    second_hat = new_second / (1.0 - beta_second**STEP)
    new_master = master - learn_rate * (
        first_hat / (jnp.sqrt(second_hat) + adam_epsilon) + weight_decay * master
    )
    return (new_master, new_first, new_second)


def step_kernel(
    tok_hbm,
    ups_hbm,
    om_hbm,
    of_hbm,
    os_hbm,
    gm_hbm,
    gf_hbm,
    gs_hbm,
    mask_ref,
    out_ref,
    grad_ref,
    mom_hbm,
    mas_hbm,
    mf,
    momf,
    stage_w,
    stage_m,
    W,
    T,
    acc,
    H,
    XT,
    G,
    R1,
    R2m,
    R2p,
    RY,
    RYF,
    O,
    RC,
    PT,
    RZp,
    RZm,
    RYH,
    load_sems,
    send_sems,
    a_send,
    a_recv,
    m_send,
    m_recv,
    own_sems,
    tz_recv,
    tc_recv,
    ty_recv,
    w_recv,
    r1_recv,
    r2m_recv,
    r2p_recv,
    ry_recv,
    ryf_recv,
    rc_recv,
    rzp_recv,
    rzm_recv,
    ryh_recv,
):
    f = lax.axis_index("fsdp")
    d = lax.axis_index("dp")
    x, yl = lax.div(f, 2), lax.rem(f, 2)
    yh, z, c = lax.div(d, 16), lax.rem(lax.div(d, 2), NZ), lax.rem(d, 2)

    def fs(dx, du):
        ylu = yl if du == 0 else 1 - yl
        return lax.rem(x + dx, NX) * 2 + ylu

    def dpi(dz, du, dv):
        yhu = yh if du == 0 else 1 - yh
        cv = c if dv == 0 else 1 - c
        return (yhu * NZ + lax.rem(z + dz, NZ)) * 2 + cv

    XP, XM, YP = {"fsdp": fs(1, 0)}, {"fsdp": fs(3, 0)}, {"fsdp": fs(0, 1)}
    ZP, ZM = {"dp": dpi(1, 0, 0)}, {"dp": dpi(7, 0, 0)}
    YH, CP = {"dp": dpi(0, 1, 0)}, {"dp": dpi(0, 0, 1)}

    sent = []

    def send(src, dst, rsem, dev):
        copy = pltpu.make_async_remote_copy(
            src_ref=src,
            dst_ref=dst,
            send_sem=send_sems.at[len(sent)],
            recv_sem=rsem,
            device_id=dev,
            device_id_type=MESH,
        )
        copy.start()
        sent.append(copy)

    def arrived(dst, rsem):
        pltpu.make_async_copy(dst, dst, rsem).wait()

    loads = []

    def load(src, dst):
        copy = pltpu.make_async_copy(src, dst, load_sems.at[len(loads)])
        copy.start()
        loads.append(copy)
        return copy

    n_old = om_hbm.shape[2]
    n_new = gm_hbm.shape[2]
    load_w = [
        (
            load(om_hbm.at[p], mf.at[p, :, pl.ds(0, n_old)]),
            load(gm_hbm.at[p], mf.at[p, :, pl.ds(n_old, n_new)]),
        )
        for p in range(3)
    ]

    def row(k, u, v):
        at = PLACE[k]
        return (at // 4) * 256 + v * 128 + ((at % 4) * 2 + u) * 16

    def blk(k, u, v):
        return T.at[:, pl.ds(row(k, u, v), 16), :]

    load_t = [
        load(tok_hbm, T.at[0, pl.ds(row(0, 0, 0), 16), :]),
        load(ups_hbm, T.at[1, pl.ds(row(0, 0, 0), 16), :]),
    ]
    load_m = [
        load(of_hbm, momf.at[pl.ds(0, 3), :, pl.ds(0, n_old)]),
        load(gf_hbm, momf.at[pl.ds(0, 3), :, pl.ds(n_old, n_new)]),
        load(os_hbm, momf.at[pl.ds(3, 3), :, pl.ds(0, n_old)]),
        load(gs_hbm, momf.at[pl.ds(3, 3), :, pl.ds(n_old, n_new)]),
    ]

    def other(i):
        half = lax.div(i + 1, 2)
        turn = 1 - 2 * lax.rem(i + 1, 2)
        return lax.rem(d + NDP + turn * half, NDP)

    barrier = pltpu.get_barrier_semaphore()

    def greet(i, carry):
        pl.semaphore_signal(
            barrier, inc=1, device_id={"dp": other(i)}, device_id_type=MESH
        )
        return carry

    lax.fori_loop(1, NDP, greet, 0)
    for dev in (XP, XM, YP):
        pl.semaphore_signal(barrier, inc=1, device_id=dev, device_id_type=MESH)

    def wrow(fi, lo, n):
        return pl.ds(pl.multiple_of(fi * 512 + lo, 16), n)

    def mine16(lo):
        return pl.ds(pl.multiple_of(lo + d * 16, 16), 16)

    for p in range(3):
        for copy in load_w[p]:
            copy.wait()
        for j in range(NDP):
            stage_w[p, j] = mf[p, :, j * 256 : (j + 1) * 256].astype(BF)
        W[p, mine16(f * 512), :] = stage_w[p, d]
        if p == 0:
            pl.semaphore_wait(barrier, NDP - 1 + 3)

        def give(i, carry, p=p):
            to = other(i)
            pltpu.make_async_remote_copy(
                src_ref=stage_w.at[p, to],
                dst_ref=W.at[p, mine16(f * 512), :],
                send_sem=a_send.at[p],
                recv_sem=a_recv.at[p],
                device_id={"dp": to},
                device_id_type=MESH,
            ).start()
            return carry

        lax.fori_loop(1, NDP, give, 0)

    def core_send(k, u):
        send(blk(k, u, 0), blk(k, u, 1), tc_recv.at[k, u], CP)

    def ring_up(s, u):
        a, b = (8 - s) % 8, 7 - s
        if b == 4:
            send(
                T.at[0, pl.ds(row(a, u, 0), 16), :],
                T.at[0, pl.ds(row(b, u, 0), 16), :],
                tz_recv.at[4, u],
                ZP,
            )
        else:
            send(blk(a, u, 0), blk(b, u, 0), tz_recv.at[b, u], ZP)

    def ring_down(s, u):
        a, b = s, s + 1
        if b == 4:
            send(
                T.at[1, pl.ds(row(a, u, 0), 16), :],
                T.at[1, pl.ds(row(b, u, 0), 16), :],
                tz_recv.at[8, u],
                ZM,
            )
        else:
            send(blk(a, u, 0), blk(b, u, 0), tz_recv.at[b, u], ZM)

    def ring_step(s, u):
        up, down = (8 - s) % 8, s
        arrived(blk(up, u, 0), tz_recv.at[up, u])
        ring_up(s, u)
        arrived(blk(down, u, 0), tz_recv.at[down, u])
        ring_down(s, u)
        core_send(up, u)
        core_send(down, u)

    for copy in load_t:
        copy.wait()
    send(blk(0, 0, 0), blk(0, 1, 0), ty_recv.at[0], YH)
    ring_up(0, 0)
    ring_down(0, 0)
    core_send(0, 0)

    for copy in load_m:
        copy.wait()

    def stage_moments(q, carry):
        for j in range(NDP):
            stage_m[j, q] = momf[q, :, j * 256 : (j + 1) * 256].astype(BF)
        return carry

    lax.fori_loop(0, 6, stage_moments, 0)

    def wb(p, dx, du, lo=0, n=512):
        return W.at[p, wrow(fs(dx, du), lo, n), :]

    def w_own(p):
        arrived(W.at[p, wrow(f, 0, 496), :], a_recv.at[p])
        send(wb(p, 0, 0), wb(p, 0, 0), w_recv.at[p, 2], YP)
        send(wb(p, 0, 0), wb(p, 0, 0), w_recv.at[p, 0], XP)
        send(wb(p, 0, 0), wb(p, 0, 0), w_recv.at[p, 1], XM)

    def w_partner(p):
        arrived(wb(p, 0, 1), w_recv.at[p, 2])
        if p < 2:
            send(wb(p, 0, 1), wb(p, 0, 1), w_recv.at[p, 3], XP)
            send(wb(p, 0, 1), wb(p, 0, 1), w_recv.at[p, 4], XM)

    def w_relay(p, du):
        arrived(wb(p, 3, du), w_recv.at[p, 3 * du])
        send(wb(p, 3, du, 0, 256), wb(p, 3, du, 0, 256), w_recv.at[p, 5 + 2 * du], XP)
        if p == 2:
            send(wb(p, 3, 0), wb(p, 3, 0), w_recv.at[p, 3], YP)
        arrived(wb(p, 1, du), w_recv.at[p, 3 * du + 1])
        send(wb(p, 1, du, 256, 256), wb(p, 1, du, 256, 256), w_recv.at[p, 6 + 2 * du], XM)
        if p == 2:
            send(wb(p, 1, 0), wb(p, 1, 0), w_recv.at[p, 4], YP)

    def w_far(p, du):
        arrived(wb(p, 2, du, 0, 256), w_recv.at[p, 5 + 2 * du])
        arrived(wb(p, 2, du, 256, 256), w_recv.at[p, 6 + 2 * du])

    w_own(0)
    arrived(blk(0, 1, 0), ty_recv.at[0])
    ring_up(0, 1)
    ring_down(0, 1)
    core_send(0, 1)
    w_own(1)
    w_partner(0)
    w_own(2)
    keep = pltpu.make_async_copy(W.at[:, wrow(f, 0, 512), :], mas_hbm, own_sems.at[0])
    keep.start()
    w_partner(1)
    ring_step(1, 0)
    w_relay(0, 0)
    w_relay(0, 1)
    ring_step(1, 1)
    w_relay(1, 0)
    w_partner(2)
    w_relay(2, 0)
    ring_step(2, 0)
    w_relay(1, 1)
    ring_step(2, 1)
    ring_step(3, 0)
    w_far(2, 0)
    send(wb(2, 2, 0), wb(2, 2, 0), w_recv.at[2, 7], YP)
    ring_step(3, 1)

    def give_moments(i, carry):
        to = other(i)
        pltpu.make_async_remote_copy(
            src_ref=stage_m.at[to],
            dst_ref=mom_hbm.at[:, mine16(0), :],
            send_sem=m_send.at[0],
            recv_sem=m_recv.at[0],
            device_id={"dp": to},
            device_id_type=MESH,
        ).start()
        return carry

    lax.fori_loop(1, NDP, give_moments, 0)
    keep_m = pltpu.make_async_copy(stage_m.at[d], mom_hbm.at[:, mine16(0), :], own_sems.at[1])
    keep_m.start()

    first_ones = NDP * n_old // (n_old + n_new)
    grown_at = jnp.maximum(d - first_ones, 0) * 256
    grown_scale = mask_ref[:, pl.ds(pl.multiple_of(grown_at, 256), 256)]
    is_grown = jnp.where(d >= first_ones, 1.0, 0.0)
    scale = is_grown * grown_scale + (1.0 - is_grown)

    def project(h, p):
        left = T[0 if p < 2 else 1, h * 256 : (h + 1) * 256, :]
        acc[p] = jnp.dot(left, W[p], preferred_element_type=F32)

    def pointwise(h):
        gate_value, up_value = acc[0], acc[1]
        sigmoid_gate = jax.nn.sigmoid(gate_value)
        activated = gate_value * sigmoid_gate
        hidden = activated * up_value * scale
        back_hidden = acc[2] * scale
        gate_back = (
            back_hidden * up_value * sigmoid_gate * (1.0 + gate_value * (1.0 - sigmoid_gate))
        )
        up_back = back_hidden * activated
        rounded = hidden.astype(BF)
        H[0, h * 128 : (h + 1) * 128] = rounded[:128]
        H[1, h * 128 : (h + 1) * 128] = rounded[128:]
        cols = slice(h * 256, (h + 1) * 256)
        XT[0:256, cols] = gate_back.T.astype(BF)
        XT[256:512, cols] = up_back.T.astype(BF)
        XT[512:768, cols] = hidden.T.astype(BF)

    for k in (0, 1, 7, 2):
        for u in (0, 1):
            arrived(blk(k, u, 1), tc_recv.at[k, u])
    w_far(0, 0)
    w_far(0, 1)
    project(0, 0)
    w_far(1, 0)
    w_far(1, 1)
    project(0, 1)
    for u in (0, 1):
        arrived(T.at[0, pl.ds(row(4, u, 0), 16), :], tz_recv.at[4, u])
        arrived(T.at[1, pl.ds(row(4, u, 0), 16), :], tz_recv.at[8, u])
        core_send(4, u)
    arrived(wb(2, 3, 1), w_recv.at[2, 3])
    arrived(wb(2, 1, 1), w_recv.at[2, 4])
    arrived(wb(2, 2, 1), w_recv.at[2, 7])
    project(0, 2)
    pointwise(0)
    for k in (6, 3, 5, 4):
        for u in (0, 1):
            arrived(blk(k, u, 1), tc_recv.at[k, u])
    project(1, 0)
    project(1, 1)
    project(1, 2)
    pointwise(1)

    def tcols(i, fi):
        return T[i, :, pl.ds(pl.multiple_of(fi * 512, 512), 512)]

    def grad_gu(dx, du):
        G[dx, du, 0:512] = jnp.dot(
            XT[0:512], tcols(0, fs(dx, du)), preferred_element_type=F32
        ).astype(BF)

    def grad_down(dx, du):
        G[dx, du, 512:768] = jnp.dot(
            XT[512:768], tcols(1, fs(dx, du)), preferred_element_type=F32
        ).astype(BF)

    def out_part(v):
        def chunk(j, carry):
            cols = pl.ds(pl.multiple_of(j * 512, 512), 512)
            O[v, :, cols] = lax.dot_general(
                H[v],
                W[2, cols, :],
                (((1,), (1,)), ((), ())),
                preferred_element_type=F32,
            ).astype(BF)
            return carry

        lax.fori_loop(0, 8, chunk, 0)

    def g_first(g, du, lo, n):
        a, b = pl.ds(lo, n // 2), pl.ds(lo + n // 2, n // 2)
        send(G.at[2, du, a, :], R1.at[du, a, :], r1_recv.at[g, 0], XP)
        send(G.at[2, du, b, :], R1.at[du, b, :], r1_recv.at[g, 1], XM)

    def g_second(g, du, lo, n):
        a, b = pl.ds(lo, n // 2), pl.ds(lo + n // 2, n // 2)
        arrived(R1.at[du, a, :], r1_recv.at[g, 0])
        G[1, du, a, :] = (G[1, du, a, :].astype(F32) + R1[du, a, :].astype(F32)).astype(BF)
        w = pl.ds(lo, n)
        send(G.at[1, du, w, :], R2m.at[du, w, :], r2m_recv.at[g], XP)
        arrived(R1.at[du, b, :], r1_recv.at[g, 1])
        G[3, du, b, :] = (G[3, du, b, :].astype(F32) + R1[du, b, :].astype(F32)).astype(BF)
        send(G.at[3, du, w, :], R2p.at[du, w, :], r2p_recv.at[g], XM)

    def g_third(g, du, lo, n):
        w = pl.ds(lo, n)
        arrived(R2m.at[du, w, :], r2m_recv.at[g])
        arrived(R2p.at[du, w, :], r2p_recv.at[g])
        return (
            G[0, du, w, :].astype(F32) + R2m[du, w, :].astype(F32) + R2p[du, w, :].astype(F32)
        )

    grad_gu(2, 1)
    g_first(1, 1, 0, 512)
    for dx in (2, 1, 3, 0):
        grad_down(dx, 1)
        send(G.at[dx, 1, pl.ds(512, 256), :], RYF.at[dx], ryf_recv.at[dx], YP)
    grad_gu(2, 0)
    g_first(0, 0, 0, 512)
    out_part(1)
    for h in (0, 1):
        rows = pl.ds(h * 128, 128)
        send(O.at[1, rows, :], RC.at[rows, :], rc_recv.at[h], CP)

    def down_sum(dx):
        arrived(RYF.at[dx], ryf_recv.at[dx])
        G[dx, 0, 512:768, :] = (
            jnp.dot(XT[512:768], tcols(1, fs(dx, 0)), preferred_element_type=F32)
            .astype(BF)
            .astype(F32)
            + RYF[dx].astype(F32)
        ).astype(BF)

    down_sum(2)
    g_first(2, 0, 512, 256)
    out_part(0)
    grad_gu(1, 1)
    grad_gu(3, 1)

    def zrows(k):
        return pl.ds(PLACE[k] * 32, 32)

    def core_sum(h):
        rows = pl.ds(h * 128, 128)
        arrived(RC.at[rows, :], rc_recv.at[h])
        PT[rows, :] = (O[0, rows, :].astype(F32) + RC[rows, :].astype(F32)).astype(BF)

    core_sum(1)
    left, right = pl.ds(0, 2048), pl.ds(2048, 2048)
    send(PT.at[zrows(4), left], RZp.at[0, :, left], rzp_recv.at[0], ZP)
    send(PT.at[zrows(4), right], RZm.at[0, :, right], rzm_recv.at[0], ZM)
    core_sum(0)

    def z_step(s):
        whole = pl.ds(0, 4096)
        for k, got, sem, cols, to in (
            (4 - s, RZp, rzp_recv, left if s == 1 else whole, ZP),
            (4 + s, RZm, rzm_recv, right if s == 1 else whole, ZM),
        ):
            arrived(got.at[s - 1, :, cols], sem.at[s - 1])
            PT[zrows(k), cols] = (
                PT[zrows(k), cols].astype(F32) + got[s - 1, :, cols].astype(F32)
            ).astype(BF)
            send(PT.at[zrows(k), :], got.at[s], sem.at[s], to)

    g_second(1, 1, 0, 512)
    z_step(1)
    grad_gu(1, 0)
    grad_gu(3, 0)
    g_second(0, 0, 0, 512)
    z_step(2)
    down_sum(1)
    down_sum(3)
    g_second(2, 0, 512, 256)
    grad_gu(0, 1)
    grad_gu(0, 0)
    down_sum(0)
    z_step(3)

    G[0, 1, 0:512] = g_third(1, 1, 0, 512).astype(BF)
    send(G.at[0, 1, pl.ds(0, 512), :], RY, ry_recv.at[0], YP)

    arrived(RZp.at[3], rzp_recv.at[3])
    arrived(RZm.at[3], rzm_recv.at[3])
    near = PT[zrows(0), :].astype(F32) + RZp[3].astype(F32) + RZm[3].astype(F32)
    PT[16:32, :] = near[16:].astype(BF)
    send(PT.at[pl.ds(16, 16), :], RYH, ryh_recv.at[0], YH)

    grad_ref[2] = g_third(2, 0, 512, 256).T
    both = g_third(0, 0, 0, 512)
    arrived(RYH, ryh_recv.at[0])
    out_ref[...] = (near[:16] + RYH[...].astype(F32)).astype(BF)
    arrived(RY, ry_recv.at[0])
    both = both + RY[...].astype(F32)
    grad_ref[0] = both[:256].T
    grad_ref[1] = both[256:].T

    arrived(mom_hbm.at[:, pl.ds(0, 496), :], m_recv.at[0])
    for p in range(3):
        pltpu.make_async_copy(
            stage_w.at[p, pl.ds(0, 31)], stage_w.at[p, pl.ds(0, 31)], a_send.at[p]
        ).wait()
    pltpu.make_async_copy(
        stage_m.at[pl.ds(0, 31)], stage_m.at[pl.ds(0, 31)], m_send.at[0]
    ).wait()
    keep.wait()
    keep_m.wait()
    for copy in sent:
        copy.wait_send()


def local(
    tokens,
    upstream,
    old_master,
    old_first,
    old_second,
    grown_master,
    grown_first,
    grown_second,
    grow_mask,
):
    planes = tuple(
        jnp.transpose(a, (1, 0, 2))
        for a in (old_master, old_first, old_second, grown_master, grown_first, grown_second)
    )
    anyspace = pl.BlockSpec(memory_space=pl.ANY)
    vmem = pl.BlockSpec(memory_space=pltpu.VMEM)
    dma = pltpu.SemaphoreType.DMA
    out, gradients, moments, master = pl.pallas_call(
        step_kernel,
        out_shape=(
            jax.ShapeDtypeStruct((16, 4096), BF),
            jax.ShapeDtypeStruct((3, 512, 256), F32),
            jax.ShapeDtypeStruct((6, 512, 256), BF),
            jax.ShapeDtypeStruct((3, 512, 256), BF),
        ),
        in_specs=[anyspace] * 8 + [vmem],
        out_specs=(vmem, vmem, anyspace, anyspace),
        scratch_shapes=[
            pltpu.VMEM((3, 16, 8192), F32),
            pltpu.VMEM((6, 16, 8192), F32),
            pltpu.VMEM((3, 32, 16, 256), BF),
            pltpu.VMEM((32, 6, 16, 256), BF),
            pltpu.VMEM((3, 4096, 256), BF),
            pltpu.VMEM((2, 512, 4096), BF),
            pltpu.VMEM((3, 256, 256), F32),
            pltpu.VMEM((2, 256, 256), BF),
            pltpu.VMEM((768, 512), BF),
            pltpu.VMEM((4, 2, 768, 512), BF),
            pltpu.VMEM((2, 768, 512), BF),
            pltpu.VMEM((2, 768, 512), BF),
            pltpu.VMEM((2, 768, 512), BF),
            pltpu.VMEM((512, 512), BF),
            pltpu.VMEM((4, 256, 512), BF),
            pltpu.VMEM((2, 256, 4096), BF),
            pltpu.VMEM((256, 4096), BF),
            pltpu.VMEM((256, 4096), BF),
            pltpu.VMEM((4, 32, 4096), BF),
            pltpu.VMEM((4, 32, 4096), BF),
            pltpu.VMEM((16, 4096), BF),
            dma((12,)),
            dma((96,)),
            dma((3,)),
            dma((3,)),
            dma((1,)),
            dma((1,)),
            dma((2,)),
            dma((9, 2)),
            dma((8, 2)),
            dma((1,)),
            dma((3, 9)),
            dma((3, 2)),
            dma((3,)),
            dma((3,)),
            dma((1,)),
            dma((4,)),
            dma((2,)),
            dma((4,)),
            dma((4,)),
            dma((1,)),
        ],
        compiler_params=pltpu.CompilerParams(
            collective_id=0, has_side_effects=True, vmem_limit_bytes=64000 * 1024
        ),
        name="grown_step",
    )(tokens, upstream, *planes, grow_mask.reshape(1, -1))
    moments = moments.astype(F32)
    updated = adam_update(master.astype(F32), moments[:3], moments[3:], gradients)
    return (out,) + tuple(jnp.transpose(a, (1, 0, 2)) for a in updated)


def solution(mesh):
    rows = P(("fsdp", "dp"), None)
    stored = P(("fsdp", "dp"), None, None)
    owned = P("fsdp", None, "dp")
    return jax.shard_map(
        local,
        mesh=mesh,
        in_specs=(rows, rows) + (stored,) * 6 + (P(),),
        out_specs=(rows, owned, owned, owned),
        check_vma=False,
    )
```

```python
import functools

import jax
import jax.numpy as jnp
from jax import lax
from jax.experimental import pallas as pl
from jax.experimental.pallas import tpu as pltpu
from jax.sharding import PartitionSpec as P

STEP = 1000

beta_first = 0.9
beta_second = 0.999
adam_epsilon = 1e-08
learn_rate = 0.001
weight_decay = 0.1

BF = jnp.bfloat16
F32 = jnp.float32
MESH = pl.DeviceIdType.MESH

NX, NZ, NDP = 4, 8, 32
MOMENTS = (16, 22, 25, 28, 30, 32, 32)
PLACE = {k: i for i, k in enumerate((0, 1, 7, 2, 6, 3, 5, 4))}


def adam_update(master, first_moment, second_moment, gradients):
    new_first = beta_first * first_moment + (1.0 - beta_first) * gradients
    new_second = beta_second * second_moment + (1.0 - beta_second) * gradients * gradients
    first_hat = new_first / (1.0 - beta_first**STEP)
    second_hat = new_second / (1.0 - beta_second**STEP)
    new_master = master - learn_rate * (
        first_hat / (jnp.sqrt(second_hat) + adam_epsilon) + weight_decay * master
    )
    return (new_master, new_first, new_second)


def step_kernel(
    tok_hbm,
    ups_hbm,
    om_hbm,
    of_hbm,
    os_hbm,
    gm_hbm,
    gf_hbm,
    gs_hbm,
    mask_ref,
    out_ref,
    grad_ref,
    fst_hbm,
    snd_hbm,
    mas_hbm,
    mf,
    momf,
    stage_w,
    stage_m,
    W,
    T,
    acc,
    H,
    XT,
    G,
    R1,
    R2m,
    R2p,
    RY,
    RYF,
    O,
    RC,
    PT,
    RZp,
    RZm,
    RYH,
    load_sems,
    send_sems,
    a_send,
    a_recv,
    m_send,
    m_recv,
    own_sems,
    tz_recv,
    tc_recv,
    ty_recv,
    w_recv,
    r1_recv,
    r2m_recv,
    r2p_recv,
    ry_recv,
    ryf_recv,
    rc_recv,
    rzp_recv,
    rzm_recv,
    ryh_recv,
):
    f = lax.axis_index("fsdp")
    d = lax.axis_index("dp")
    x, yl = lax.div(f, 2), lax.rem(f, 2)
    yh, z, c = lax.div(d, 16), lax.rem(lax.div(d, 2), NZ), lax.rem(d, 2)

    def fs(dx, du):
        ylu = yl if du == 0 else 1 - yl
        return lax.rem(x + dx, NX) * 2 + ylu

    def dpi(dz, du, dv):
        yhu = yh if du == 0 else 1 - yh
        cv = c if dv == 0 else 1 - c
        return (yhu * NZ + lax.rem(z + dz, NZ)) * 2 + cv

    XP, XM, YP = {"fsdp": fs(1, 0)}, {"fsdp": fs(3, 0)}, {"fsdp": fs(0, 1)}
    ZP, ZM = {"dp": dpi(1, 0, 0)}, {"dp": dpi(7, 0, 0)}
    CP = {"dp": dpi(0, 0, 1)}
    YN = {"dp": dpi(0, 1, 0), "fsdp": fs(0, 1)}

    sent = []

    def send(src, dst, rsem, dev):
        copy = pltpu.make_async_remote_copy(
            src_ref=src,
            dst_ref=dst,
            send_sem=send_sems.at[len(sent)],
            recv_sem=rsem,
            device_id=dev,
            device_id_type=MESH,
        )
        copy.start()
        sent.append(copy)

    def arrived(dst, rsem):
        pltpu.make_async_copy(dst, dst, rsem).wait()

    loads = []

    def load(src, dst):
        copy = pltpu.make_async_copy(src, dst, load_sems.at[len(loads)])
        copy.start()
        loads.append(copy)
        return copy

    n_old = om_hbm.shape[2]
    n_new = gm_hbm.shape[2]
    load_w = [
        (
            load(om_hbm.at[p], mf.at[p, :, pl.ds(0, n_old)]),
            load(gm_hbm.at[p], mf.at[p, :, pl.ds(n_old, n_new)]),
        )
        for p in range(3)
    ]

    def row(k, u, v):
        at = PLACE[k]
        return (at // 4) * 256 + v * 128 + ((at % 4) * 2 + u) * 16

    def blk(k, u, v):
        return T.at[:, pl.ds(row(k, u, v), 16), :]

    load_t = [
        load(tok_hbm, T.at[0, pl.ds(row(0, 0, 0), 16), :]),
        load(ups_hbm, T.at[1, pl.ds(row(0, 0, 0), 16), :]),
    ]
    load_m = [
        load(of_hbm, momf.at[pl.ds(0, 3), :, pl.ds(0, n_old)]),
        load(gf_hbm, momf.at[pl.ds(0, 3), :, pl.ds(n_old, n_new)]),
        load(os_hbm, momf.at[pl.ds(3, 3), :, pl.ds(0, n_old)]),
        load(gs_hbm, momf.at[pl.ds(3, 3), :, pl.ds(n_old, n_new)]),
    ]

    def other(i):
        half = lax.div(i + 1, 2)
        turn = 1 - 2 * lax.rem(i + 1, 2)
        return lax.rem(d + NDP + turn * half, NDP)

    barrier = pltpu.get_barrier_semaphore()

    def greet(i, carry):
        pl.semaphore_signal(
            barrier, inc=1, device_id={"dp": other(i)}, device_id_type=MESH
        )
        return carry

    lax.fori_loop(1, NDP, greet, 0)
    for dev in (XP, XM, YP, YN):
        pl.semaphore_signal(barrier, inc=1, device_id=dev, device_id_type=MESH)

    def wrow(fi, lo, n):
        return pl.ds(pl.multiple_of(fi * 512 + lo, 16), n)

    def mine16(lo):
        return pl.ds(pl.multiple_of(lo + d * 16, 16), 16)

    for p in range(3):
        for copy in load_w[p]:
            copy.wait()
        for j in range(NDP):
            stage_w[p, j] = mf[p, :, j * 256 : (j + 1) * 256].astype(BF)
        W[p, mine16(f * 512), :] = stage_w[p, d]
        if p == 0:
            pl.semaphore_wait(barrier, NDP - 1 + 4)

        def give(i, carry, p=p):
            to = other(i)
            pltpu.make_async_remote_copy(
                src_ref=stage_w.at[p, to],
                dst_ref=W.at[p, mine16(f * 512), :],
                send_sem=a_send.at[p],
                recv_sem=a_recv.at[p],
                device_id={"dp": to},
                device_id_type=MESH,
            ).start()
            return carry

        lax.fori_loop(1, NDP, give, 0)

    def piece(i, k, u, v=0):
        return T.at[i, pl.ds(row(k, u, v), 16), :]

    def core_send(i, k, u):
        send(piece(i, k, u), piece(i, k, u, 1), tc_recv.at[k, u, i], CP)

    def side_send(i, k):
        send(piece(i, k, 0), piece(i, k, 1), ty_recv.at[k, i], YN)

    left, right = pl.ds(0, 2048), pl.ds(2048, 2048)
    streams = ((0, 0), (1, 0), (0, 1))

    def ring_piece(j, k, down):
        i, u = streams[j]
        if k != 4:
            return piece(i, k, u), tz_recv.at[k, j]
        if j == 2:
            half = right if down else left
            return T.at[i, pl.ds(row(k, u, 0), 16), half], tz_recv.at[0 if down else 4, j]
        return (piece(i, k, u), tz_recv.at[4, j]) if j == down else (None, None)

    def ring_send(j, s, down):
        a, b = (s, s + 1) if down else ((8 - s) % 8, 7 - s)
        dst, sem = ring_piece(j, b, down)
        if dst is None:
            return
        i, u = streams[j]
        src = piece(i, a, u)
        if b == 4 and j == 2:
            src = T.at[i, pl.ds(row(a, u, 0), 16), right if down else left]
        send(src, dst, sem, ZM if down else ZP)

    def ring_step(s):
        for j, (i, u) in enumerate(streams):
            for down in (0, 1):
                k = s if down else (8 - s) % 8
                arrived(piece(i, k, u), tz_recv.at[k, j])
                ring_send(j, s, down)
            for k in ((8 - s) % 8, s):
                if j == 1:
                    side_send(1, k)
                core_send(i, k, u)

    def side_arrived(k):
        arrived(piece(1, k, 1), ty_recv.at[k, 1])
        core_send(1, k, 1)

    for copy in load_t:
        copy.wait()
    for i in (0, 1):
        side_send(i, 0)
        for down in (0, 1):
            ring_send(i, 0, down)
        core_send(i, 0, 0)

    for copy in load_m:
        copy.wait()

    def stage_moments(q, carry):
        for j in range(NDP):
            stage_m[j, q] = momf[q, :, j * 256 : (j + 1) * 256].astype(BF)
        return carry

    lax.fori_loop(0, 6, stage_moments, 0)

    def wb(p, dx, du, lo=0, n=512):
        return W.at[p, wrow(fs(dx, du), lo, n), :]

    def w_own(p):
        arrived(W.at[p, wrow(f, 0, 496), :], a_recv.at[p])
        send(wb(p, 0, 0), wb(p, 0, 0), w_recv.at[p, 2], YP)
        send(wb(p, 0, 0), wb(p, 0, 0), w_recv.at[p, 0], XP)
        send(wb(p, 0, 0), wb(p, 0, 0), w_recv.at[p, 1], XM)

    def w_partner(p):
        arrived(wb(p, 0, 1), w_recv.at[p, 2])
        if p < 2:
            send(wb(p, 0, 1), wb(p, 0, 1), w_recv.at[p, 3], XP)
            send(wb(p, 0, 1), wb(p, 0, 1), w_recv.at[p, 4], XM)

    def w_relay(p, du):
        arrived(wb(p, 3, du), w_recv.at[p, 3 * du])
        send(wb(p, 3, du, 0, 256), wb(p, 3, du, 0, 256), w_recv.at[p, 5 + 2 * du], XP)
        if p == 2:
            send(wb(p, 3, 0), wb(p, 3, 0), w_recv.at[p, 3], YP)
        arrived(wb(p, 1, du), w_recv.at[p, 3 * du + 1])
        send(wb(p, 1, du, 256, 256), wb(p, 1, du, 256, 256), w_recv.at[p, 6 + 2 * du], XM)
        if p == 2:
            send(wb(p, 1, 0), wb(p, 1, 0), w_recv.at[p, 4], YP)

    def w_far(p, du):
        arrived(wb(p, 2, du, 0, 256), w_recv.at[p, 5 + 2 * du])
        arrived(wb(p, 2, du, 256, 256), w_recv.at[p, 6 + 2 * du])

    w_own(0)
    arrived(piece(0, 0, 1), ty_recv.at[0, 0])
    for down in (0, 1):
        ring_send(2, 0, down)
    core_send(0, 0, 1)
    side_arrived(0)
    w_own(1)
    w_partner(0)
    w_own(2)
    keep = pltpu.make_async_copy(W.at[:, wrow(f, 0, 512), :], mas_hbm, own_sems.at[0])
    keep.start()
    ring_step(1)
    w_partner(1)
    w_relay(0, 0)
    ring_step(2)
    w_relay(2, 0)
    w_relay(0, 1)
    w_relay(1, 0)
    ring_step(3)
    w_relay(1, 1)
    w_partner(2)

    def give_moments(i, carry):
        r = lax.rem(i, 16)
        turn = (1 - 2 * lax.rem(r + 1, 2)) * lax.div(r + 1, 2)
        there = yh + lax.div(i, 16) * (1 - 2 * yh)
        to = there * 16 + lax.rem(lax.rem(d, 16) + 16 + turn, 16)
        for half, dst in enumerate((fst_hbm, snd_hbm)):
            pltpu.make_async_remote_copy(
                src_ref=stage_m.at[to, pl.ds(3 * half, 3)],
                dst_ref=dst.at[:, mine16(0), :],
                send_sem=m_send.at[half],
                recv_sem=m_recv.at[half],
                device_id={"dp": to},
                device_id_type=MESH,
            ).start()
        return carry

    given = [1]

    def moments_to(n):
        lax.fori_loop(given[0], n, give_moments, 0)
        given[0] = n

    keep_m = [
        pltpu.make_async_copy(
            stage_m.at[d, pl.ds(3 * half, 3)], dst.at[:, mine16(0), :], own_sems.at[1 + half]
        )
        for half, dst in enumerate((fst_hbm, snd_hbm))
    ]
    for copy in keep_m:
        copy.start()
    moments_to(MOMENTS[0])

    side_arrived(7)
    side_arrived(1)
    side_arrived(6)
    side_arrived(2)
    arrived(piece(0, 4, 0), tz_recv.at[4, 0])
    core_send(0, 4, 0)
    arrived(piece(1, 4, 0), tz_recv.at[4, 1])
    side_send(1, 4)
    core_send(1, 4, 0)
    side_arrived(5)
    side_arrived(3)
    for down in (0, 1):
        arrived(*ring_piece(2, 4, down))
    core_send(0, 4, 1)

    first_ones = NDP * n_old // (n_old + n_new)
    grown_at = jnp.maximum(d - first_ones, 0) * 256
    grown_scale = mask_ref[:, pl.ds(pl.multiple_of(grown_at, 256), 256)]
    is_grown = jnp.where(d >= first_ones, 1.0, 0.0)
    scale = is_grown * grown_scale + (1.0 - is_grown)

    near, far = ((0, 0), (0, 1), (1, 0), (3, 0), (1, 1), (3, 1)), ((2, 0), (2, 1))

    def project(p, blocks, start):
        for h in (0, 1):
            total = None if start else acc[h, p]
            for dx, du in blocks:
                fi = fs(dx, du)
                at = pl.ds(pl.multiple_of(fi * 512, 512), 512)
                part = jnp.dot(
                    T[0 if p < 2 else 1, h * 256 : (h + 1) * 256, at],
                    W[p, at, :],
                    preferred_element_type=F32,
                )
                total = part if total is None else total + part
            acc[h, p] = total

    def pointwise(h):
        gate_value, up_value = acc[h, 0], acc[h, 1]
        sigmoid_gate = jax.nn.sigmoid(gate_value)
        activated = gate_value * sigmoid_gate
        hidden = activated * up_value * scale
        back_hidden = acc[h, 2] * scale
        gate_back = (
            back_hidden * up_value * sigmoid_gate * (1.0 + gate_value * (1.0 - sigmoid_gate))
        )
        up_back = back_hidden * activated
        rounded = hidden.astype(BF)
        H[0, h * 128 : (h + 1) * 128] = rounded[:128]
        H[1, h * 128 : (h + 1) * 128] = rounded[128:]
        cols = slice(h * 256, (h + 1) * 256)
        XT[0:256, cols] = gate_back.T.astype(BF)
        XT[256:512, cols] = up_back.T.astype(BF)
        XT[512:768, cols] = hidden.T.astype(BF)

    for i in (0, 1):
        for k in (0, 1, 7, 2, 6, 3, 5, 4):
            for u in (0, 1):
                if (i, k, u) != (1, 4, 1):
                    arrived(piece(i, k, u, 1), tc_recv.at[k, u, i])
    project(0, near, True)
    w_far(2, 0)
    send(wb(2, 2, 0), wb(2, 2, 0), w_recv.at[2, 7], YP)
    moments_to(MOMENTS[1])
    project(1, near, True)
    w_far(0, 0)
    w_far(0, 1)
    project(0, far, False)
    arrived(wb(2, 3, 1), w_recv.at[2, 3])
    arrived(wb(2, 1, 1), w_recv.at[2, 4])
    side_arrived(4)
    arrived(piece(1, 4, 1, 1), tc_recv.at[4, 1, 1])
    project(2, near, True)
    w_far(1, 0)
    w_far(1, 1)
    project(1, far, False)
    arrived(wb(2, 2, 1), w_recv.at[2, 7])
    project(2, far, False)
    pointwise(0)
    pointwise(1)

    def tcols(i, fi):
        return T[i, :, pl.ds(pl.multiple_of(fi * 512, 512), 512)]

    def grad_gu(dx, du):
        G[dx, du, 0:512] = jnp.dot(
            XT[0:512], tcols(0, fs(dx, du)), preferred_element_type=F32
        ).astype(BF)

    def grad_down(dx, du):
        G[dx, du, 512:768] = jnp.dot(
            XT[512:768], tcols(1, fs(dx, du)), preferred_element_type=F32
        ).astype(BF)

    def out_part(v):
        def chunk(j, carry):
            cols = pl.ds(pl.multiple_of(j * 512, 512), 512)
            O[v, :, cols] = lax.dot_general(
                H[v],
                W[2, cols, :],
                (((1,), (1,)), ((), ())),
                preferred_element_type=F32,
            ).astype(BF)
            return carry

        lax.fori_loop(0, 8, chunk, 0)

    def g_first(g, du, lo, n):
        a, b = pl.ds(lo, n // 2), pl.ds(lo + n // 2, n // 2)
        send(G.at[2, du, a, :], R1.at[du, a, :], r1_recv.at[g, 0], XP)
        send(G.at[2, du, b, :], R1.at[du, b, :], r1_recv.at[g, 1], XM)

    def g_second(g, du, lo, n):
        a, b = pl.ds(lo, n // 2), pl.ds(lo + n // 2, n // 2)
        arrived(R1.at[du, a, :], r1_recv.at[g, 0])
        G[1, du, a, :] = (G[1, du, a, :].astype(F32) + R1[du, a, :].astype(F32)).astype(BF)
        w = pl.ds(lo, n)
        send(G.at[1, du, w, :], R2m.at[du, w, :], r2m_recv.at[g], XP)
        arrived(R1.at[du, b, :], r1_recv.at[g, 1])
        G[3, du, b, :] = (G[3, du, b, :].astype(F32) + R1[du, b, :].astype(F32)).astype(BF)
        send(G.at[3, du, w, :], R2p.at[du, w, :], r2p_recv.at[g], XM)

    def g_third(g, du, lo, n):
        w = pl.ds(lo, n)
        arrived(R2m.at[du, w, :], r2m_recv.at[g])
        arrived(R2p.at[du, w, :], r2p_recv.at[g])
        return (
            G[0, du, w, :].astype(F32) + R2m[du, w, :].astype(F32) + R2p[du, w, :].astype(F32)
        )

    grad_gu(2, 1)
    g_first(1, 1, 0, 512)
    grad_gu(2, 0)
    g_first(0, 0, 0, 512)
    out_part(1)
    for h in (0, 1):
        rows = pl.ds(h * 128, 128)
        send(O.at[1, rows, :], RC.at[rows, :], rc_recv.at[h], CP)
    for dx in (2, 1, 3, 0):
        grad_down(dx, 1)
        send(G.at[dx, 1, pl.ds(512, 256), :], RYF.at[dx], ryf_recv.at[dx], YP)
    out_part(0)

    def down_sum(dx):
        arrived(RYF.at[dx], ryf_recv.at[dx])
        G[dx, 0, 512:768, :] = (
            jnp.dot(XT[512:768], tcols(1, fs(dx, 0)), preferred_element_type=F32)
            .astype(BF)
            .astype(F32)
            + RYF[dx].astype(F32)
        ).astype(BF)

    def zrows(k):
        return pl.ds(PLACE[k] * 32, 32)

    def core_sum(h):
        rows = pl.ds(h * 128, 128)
        arrived(RC.at[rows, :], rc_recv.at[h])
        PT[rows, :] = (O[0, rows, :].astype(F32) + RC[rows, :].astype(F32)).astype(BF)

    core_sum(1)
    send(PT.at[zrows(4), left], RZp.at[0, :, left], rzp_recv.at[0], ZP)
    send(PT.at[zrows(4), right], RZm.at[0, :, right], rzm_recv.at[0], ZM)
    moments_to(MOMENTS[2])
    core_sum(0)
    down_sum(2)
    g_first(2, 0, 512, 256)
    grad_gu(1, 1)
    grad_gu(3, 1)

    def z_step(s):
        whole = pl.ds(0, 4096)
        for k, got, sem, cols, to in (
            (4 - s, RZp, rzp_recv, left if s == 1 else whole, ZP),
            (4 + s, RZm, rzm_recv, right if s == 1 else whole, ZM),
        ):
            arrived(got.at[s - 1, :, cols], sem.at[s - 1])
            PT[zrows(k), cols] = (
                PT[zrows(k), cols].astype(F32) + got[s - 1, :, cols].astype(F32)
            ).astype(BF)
            send(PT.at[zrows(k), :], got.at[s], sem.at[s], to)

    g_second(1, 1, 0, 512)
    z_step(1)
    moments_to(MOMENTS[3])
    grad_gu(1, 0)
    grad_gu(3, 0)
    g_second(0, 0, 0, 512)
    z_step(2)
    moments_to(MOMENTS[4])
    down_sum(1)
    down_sum(3)
    g_second(2, 0, 512, 256)
    grad_gu(0, 1)
    grad_gu(0, 0)
    down_sum(0)
    z_step(3)
    moments_to(MOMENTS[5])

    G[0, 1, 0:512] = g_third(1, 1, 0, 512).astype(BF)
    send(G.at[0, 1, pl.ds(0, 512), :], RY, ry_recv.at[0], YP)

    arrived(RZp.at[3], rzp_recv.at[3])
    arrived(RZm.at[3], rzm_recv.at[3])
    nearby = PT[zrows(0), :].astype(F32) + RZp[3].astype(F32) + RZm[3].astype(F32)
    PT[16:32, :] = nearby[16:].astype(BF)
    send(PT.at[pl.ds(16, 16), :], RYH, ryh_recv.at[0], YN)
    moments_to(MOMENTS[6])

    grad_ref[2] = g_third(2, 0, 512, 256).T
    both = g_third(0, 0, 0, 512)
    arrived(RYH, ryh_recv.at[0])
    out_ref[...] = (nearby[:16] + RYH[...].astype(F32)).astype(BF)
    arrived(RY, ry_recv.at[0])
    both = both + RY[...].astype(F32)
    grad_ref[0] = both[:256].T
    grad_ref[1] = both[256:].T

    for half, dst in enumerate((fst_hbm, snd_hbm)):
        arrived(dst.at[:, pl.ds(0, 496), :], m_recv.at[half])
    for p in range(3):
        pltpu.make_async_copy(
            stage_w.at[p, pl.ds(0, 31)], stage_w.at[p, pl.ds(0, 31)], a_send.at[p]
        ).wait()
    for half in (0, 1):
        given_all = stage_m.at[pl.ds(0, 31), pl.ds(3 * half, 3)]
        pltpu.make_async_copy(given_all, given_all, m_send.at[half]).wait()
    keep.wait()
    for copy in keep_m:
        copy.wait()
    for copy in sent:
        copy.wait_send()


def local(
    tokens,
    upstream,
    old_master,
    old_first,
    old_second,
    grown_master,
    grown_first,
    grown_second,
    grow_mask,
):
    planes = tuple(
        jnp.transpose(a, (1, 0, 2))
        for a in (old_master, old_first, old_second, grown_master, grown_first, grown_second)
    )
    anyspace = pl.BlockSpec(memory_space=pl.ANY)
    vmem = pl.BlockSpec(memory_space=pltpu.VMEM)
    dma = pltpu.SemaphoreType.DMA
    out, gradients, first, second, master = pl.pallas_call(
        step_kernel,
        out_shape=(
            jax.ShapeDtypeStruct((16, 4096), BF),
            jax.ShapeDtypeStruct((3, 512, 256), F32),
            jax.ShapeDtypeStruct((3, 512, 256), BF),
            jax.ShapeDtypeStruct((3, 512, 256), BF),
            jax.ShapeDtypeStruct((3, 512, 256), BF),
        ),
        in_specs=[anyspace] * 8 + [vmem],
        out_specs=(vmem, vmem, anyspace, anyspace, anyspace),
        scratch_shapes=[
            pltpu.VMEM((3, 16, 8192), F32),
            pltpu.VMEM((6, 16, 8192), F32),
            pltpu.VMEM((3, 32, 16, 256), BF),
            pltpu.VMEM((32, 6, 16, 256), BF),
            pltpu.VMEM((3, 4096, 256), BF),
            pltpu.VMEM((2, 512, 4096), BF),
            pltpu.VMEM((2, 3, 256, 256), F32),
            pltpu.VMEM((2, 256, 256), BF),
            pltpu.VMEM((768, 512), BF),
            pltpu.VMEM((4, 2, 768, 512), BF),
            pltpu.VMEM((2, 768, 512), BF),
            pltpu.VMEM((2, 768, 512), BF),
            pltpu.VMEM((2, 768, 512), BF),
            pltpu.VMEM((512, 512), BF),
            pltpu.VMEM((4, 256, 512), BF),
            pltpu.VMEM((2, 256, 4096), BF),
            pltpu.VMEM((256, 4096), BF),
            pltpu.VMEM((256, 4096), BF),
            pltpu.VMEM((4, 32, 4096), BF),
            pltpu.VMEM((4, 32, 4096), BF),
            pltpu.VMEM((16, 4096), BF),
            dma((12,)),
            dma((160,)),
            dma((3,)),
            dma((3,)),
            dma((2,)),
            dma((2,)),
            dma((3,)),
            dma((8, 3)),
            dma((8, 2, 2)),
            dma((8, 2)),
            dma((3, 9)),
            dma((3, 2)),
            dma((3,)),
            dma((3,)),
            dma((1,)),
            dma((4,)),
            dma((2,)),
            dma((4,)),
            dma((4,)),
            dma((1,)),
        ],
        compiler_params=pltpu.CompilerParams(
            collective_id=0, has_side_effects=True, vmem_limit_bytes=64000 * 1024
        ),
        name="grown_step",
    )(tokens, upstream, *planes, grow_mask.reshape(1, -1))
    updated = adam_update(
        master.astype(F32), first.astype(F32), second.astype(F32), gradients
    )
    return (out,) + tuple(jnp.transpose(a, (1, 0, 2)) for a in updated)


def solution(mesh):
    rows = P(("fsdp", "dp"), None)
    stored = P(("fsdp", "dp"), None, None)
    owned = P("fsdp", None, "dp")
    return jax.shard_map(
        local,
        mesh=mesh,
        in_specs=(rows, rows) + (stored,) * 6 + (P(),),
        out_specs=(rows, owned, owned, owned),
        check_vma=False,
    )
```

```python
import functools

import jax
import jax.numpy as jnp
from jax import lax
from jax.experimental import pallas as pl
from jax.experimental.pallas import tpu as pltpu
from jax.sharding import PartitionSpec as P

STEP = 1000

beta_first = 0.9
beta_second = 0.999
adam_epsilon = 1e-08
learn_rate = 0.001
weight_decay = 0.1

BF = jnp.bfloat16
F32 = jnp.float32
MESH = pl.DeviceIdType.MESH

NX, NZ, NDP = 4, 8, 32
MOMENTS = (
    (0, 0), (0, 0), (0, 0), (0, 0), (15, 0), (15, 4), (15, 7), (15, 10), (15, 13), (15, 16), (15, 16),
)
PLACE = {k: i for i, k in enumerate((0, 1, 7, 2, 6, 3, 5, 4))}


def adam_update(master, first_moment, second_moment, gradients):
    new_first = beta_first * first_moment + (1.0 - beta_first) * gradients
    new_second = beta_second * second_moment + (1.0 - beta_second) * gradients * gradients
    first_hat = new_first / (1.0 - beta_first**STEP)
    second_hat = new_second / (1.0 - beta_second**STEP)
    new_master = master - learn_rate * (
        first_hat / (jnp.sqrt(second_hat) + adam_epsilon) + weight_decay * master
    )
    return (new_master, new_first, new_second)


def step_kernel(
    tok_hbm,
    ups_hbm,
    om_hbm,
    of_hbm,
    os_hbm,
    gm_hbm,
    gf_hbm,
    gs_hbm,
    mask_ref,
    out_ref,
    grad_ref,
    fst_hbm,
    snd_hbm,
    mas_hbm,
    mf,
    momf,
    stage_w,
    stage_m,
    W,
    T,
    acc,
    H,
    XT,
    G,
    R1,
    R2m,
    R2p,
    RY,
    RYS,
    RYF,
    O,
    RC,
    PT,
    RZp,
    RZm,
    RYH,
    load_sems,
    send_sems,
    a_send,
    a_recv,
    m_send,
    m_recv,
    own_sems,
    tz_recv,
    tc_recv,
    ty_recv,
    w_recv,
    r1_recv,
    r2m_recv,
    r2p_recv,
    ry_recv,
    ryf_recv,
    rc_recv,
    rzp_recv,
    rzm_recv,
    ryh_recv,
):
    f = lax.axis_index("fsdp")
    d = lax.axis_index("dp")
    x, yl = lax.div(f, 2), lax.rem(f, 2)
    yh, z, c = lax.div(d, 16), lax.rem(lax.div(d, 2), NZ), lax.rem(d, 2)

    def fs(dx, du):
        ylu = yl if du == 0 else 1 - yl
        return lax.rem(x + dx, NX) * 2 + ylu

    def dpi(dz, du, dv):
        yhu = yh if du == 0 else 1 - yh
        cv = c if dv == 0 else 1 - c
        return (yhu * NZ + lax.rem(z + dz, NZ)) * 2 + cv

    XP, XM, YP = {"fsdp": fs(1, 0)}, {"fsdp": fs(3, 0)}, {"fsdp": fs(0, 1)}
    ZP, ZM = {"dp": dpi(1, 0, 0)}, {"dp": dpi(7, 0, 0)}
    CP = {"dp": dpi(0, 0, 1)}
    YN = {"dp": dpi(0, 1, 0), "fsdp": fs(0, 1)}

    sent = []

    def send(src, dst, rsem, dev):
        copy = pltpu.make_async_remote_copy(
            src_ref=src,
            dst_ref=dst,
            send_sem=send_sems.at[len(sent)],
            recv_sem=rsem,
            device_id=dev,
            device_id_type=MESH,
        )
        copy.start()
        sent.append(copy)

    def arrived(dst, rsem):
        pltpu.make_async_copy(dst, dst, rsem).wait()

    loads = []

    def load(src, dst):
        copy = pltpu.make_async_copy(src, dst, load_sems.at[len(loads)])
        copy.start()
        loads.append(copy)
        return copy

    n_old = om_hbm.shape[2]
    n_new = gm_hbm.shape[2]
    load_w = [
        (
            load(om_hbm.at[p], mf.at[p, :, pl.ds(0, n_old)]),
            load(gm_hbm.at[p], mf.at[p, :, pl.ds(n_old, n_new)]),
        )
        for p in range(3)
    ]

    def row(k, u, v):
        at = PLACE[k]
        return (at // 4) * 256 + v * 128 + ((at % 4) * 2 + u) * 16

    def blk(k, u, v):
        return T.at[:, pl.ds(row(k, u, v), 16), :]

    load_t = [
        load(tok_hbm, T.at[0, pl.ds(row(0, 0, 0), 16), :]),
        load(ups_hbm, T.at[1, pl.ds(row(0, 0, 0), 16), :]),
    ]
    load_m = [
        load(of_hbm, momf.at[pl.ds(0, 3), :, pl.ds(0, n_old)]),
        load(gf_hbm, momf.at[pl.ds(0, 3), :, pl.ds(n_old, n_new)]),
        load(os_hbm, momf.at[pl.ds(3, 3), :, pl.ds(0, n_old)]),
        load(gs_hbm, momf.at[pl.ds(3, 3), :, pl.ds(n_old, n_new)]),
    ]

    def other(i):
        half = lax.div(i + 1, 2)
        turn = 1 - 2 * lax.rem(i + 1, 2)
        return lax.rem(d + NDP + turn * half, NDP)

    barrier = pltpu.get_barrier_semaphore()

    def greet(i, carry):
        pl.semaphore_signal(
            barrier, inc=1, device_id={"dp": other(i)}, device_id_type=MESH
        )
        return carry

    lax.fori_loop(1, NDP, greet, 0)
    for dev in (XP, XM, YP, YN):
        pl.semaphore_signal(barrier, inc=1, device_id=dev, device_id_type=MESH)

    def wrow(fi, lo, n):
        return pl.ds(pl.multiple_of(fi * 512 + lo, 16), n)

    def mine16(lo):
        return pl.ds(pl.multiple_of(lo + d * 16, 16), 16)

    for p in range(3):
        for copy in load_w[p]:
            copy.wait()
        for j in range(NDP):
            stage_w[p, j] = mf[p, :, j * 256 : (j + 1) * 256].astype(BF)
        W[p, mine16(f * 512), :] = stage_w[p, d]
        if p == 0:
            pl.semaphore_wait(barrier, NDP - 1 + 4)

        def give(i, carry, p=p):
            to = other(i)
            pltpu.make_async_remote_copy(
                src_ref=stage_w.at[p, to],
                dst_ref=W.at[p, mine16(f * 512), :],
                send_sem=a_send.at[p],
                recv_sem=a_recv.at[p],
                device_id={"dp": to},
                device_id_type=MESH,
            ).start()
            return carry

        lax.fori_loop(1, NDP, give, 0)

    def piece(i, k, u, v=0):
        return T.at[i, pl.ds(row(k, u, v), 16), :]

    def core_send(i, k, u):
        send(piece(i, k, u), piece(i, k, u, 1), tc_recv.at[k, u, i], CP)

    def side_send(i, k):
        send(piece(i, k, 0), piece(i, k, 1), ty_recv.at[k, i], YN)

    left, right = pl.ds(0, 2048), pl.ds(2048, 2048)
    streams = ((0, 0), (1, 0), (0, 1))

    def ring_piece(j, k, down):
        i, u = streams[j]
        if k != 4:
            return piece(i, k, u), tz_recv.at[k, j]
        if j == 2:
            half = right if down else left
            return T.at[i, pl.ds(row(k, u, 0), 16), half], tz_recv.at[0 if down else 4, j]
        return (piece(i, k, u), tz_recv.at[4, j]) if j == down else (None, None)

    def ring_send(j, s, down):
        a, b = (s, s + 1) if down else ((8 - s) % 8, 7 - s)
        dst, sem = ring_piece(j, b, down)
        if dst is None:
            return
        i, u = streams[j]
        src = piece(i, a, u)
        if b == 4 and j == 2:
            src = T.at[i, pl.ds(row(a, u, 0), 16), right if down else left]
        send(src, dst, sem, ZM if down else ZP)

    def ring_step(s):
        for j, (i, u) in enumerate(streams):
            for down in (0, 1):
                k = s if down else (8 - s) % 8
                arrived(piece(i, k, u), tz_recv.at[k, j])
                ring_send(j, s, down)
            for k in ((8 - s) % 8, s):
                if j == 1:
                    side_send(1, k)
                core_send(i, k, u)

    def side_arrived(k):
        arrived(piece(1, k, 1), ty_recv.at[k, 1])
        core_send(1, k, 1)

    for copy in load_t:
        copy.wait()
    for i in (0, 1):
        side_send(i, 0)
        for down in (0, 1):
            ring_send(i, 0, down)
        core_send(i, 0, 0)

    for copy in load_m:
        copy.wait()

    def stage_moments(q, carry):
        for j in range(NDP):
            stage_m[j, q] = momf[q, :, j * 256 : (j + 1) * 256].astype(BF)
        return carry

    lax.fori_loop(0, 6, stage_moments, 0)

    def wb(p, dx, du, lo=0, n=512):
        return W.at[p, wrow(fs(dx, du), lo, n), :]

    def w_own(p):
        arrived(W.at[p, wrow(f, 0, 496), :], a_recv.at[p])
        send(wb(p, 0, 0), wb(p, 0, 0), w_recv.at[p, 2], YP)
        send(wb(p, 0, 0), wb(p, 0, 0), w_recv.at[p, 0], XP)
        send(wb(p, 0, 0), wb(p, 0, 0), w_recv.at[p, 1], XM)

    def w_partner(p):
        arrived(wb(p, 0, 1), w_recv.at[p, 2])
        if p < 2:
            send(wb(p, 0, 1), wb(p, 0, 1), w_recv.at[p, 3], XP)
            send(wb(p, 0, 1), wb(p, 0, 1), w_recv.at[p, 4], XM)

    def w_relay(p, du):
        arrived(wb(p, 3, du), w_recv.at[p, 3 * du])
        send(wb(p, 3, du, 0, 256), wb(p, 3, du, 0, 256), w_recv.at[p, 5 + 2 * du], XP)
        if p == 2:
            send(wb(p, 3, 0), wb(p, 3, 0), w_recv.at[p, 3], YP)
        arrived(wb(p, 1, du), w_recv.at[p, 3 * du + 1])
        send(wb(p, 1, du, 256, 256), wb(p, 1, du, 256, 256), w_recv.at[p, 6 + 2 * du], XM)
        if p == 2:
            send(wb(p, 1, 0), wb(p, 1, 0), w_recv.at[p, 4], YP)

    def w_far(p, du):
        arrived(wb(p, 2, du, 0, 256), w_recv.at[p, 5 + 2 * du])
        arrived(wb(p, 2, du, 256, 256), w_recv.at[p, 6 + 2 * du])

    def give_moments(i, carry):
        r = lax.rem(i, 16)
        turn = (1 - 2 * lax.rem(r + 1, 2)) * lax.div(r + 1, 2)
        there = yh + lax.div(i, 16) * (1 - 2 * yh)
        to = there * 16 + lax.rem(lax.rem(d, 16) + 16 + turn, 16)
        for half, dst in enumerate((fst_hbm, snd_hbm)):
            pltpu.make_async_remote_copy(
                src_ref=stage_m.at[to, pl.ds(3 * half, 3)],
                dst_ref=dst.at[:, mine16(0), :],
                send_sem=m_send.at[half],
                recv_sem=m_recv.at[half],
                device_id={"dp": to},
                device_id_type=MESH,
            ).start()
        return carry

    given = [1, 16]

    def moments_to(point):
        for side, n in enumerate(MOMENTS[point]):
            n += 1 + 15 * side
            if n > given[side]:
                lax.fori_loop(given[side], n, give_moments, 0)
                given[side] = n

    keep_m = [
        pltpu.make_async_copy(
            stage_m.at[d, pl.ds(3 * half, 3)], dst.at[:, mine16(0), :], own_sems.at[1 + half]
        )
        for half, dst in enumerate((fst_hbm, snd_hbm))
    ]
    for copy in keep_m:
        copy.start()

    w_own(0)
    moments_to(0)
    arrived(piece(0, 0, 1), ty_recv.at[0, 0])
    for down in (0, 1):
        ring_send(2, 0, down)
    core_send(0, 0, 1)
    side_arrived(0)
    w_own(1)
    w_partner(0)
    w_own(2)
    keep = pltpu.make_async_copy(W.at[:, wrow(f, 0, 512), :], mas_hbm, own_sems.at[0])
    keep.start()
    moments_to(1)
    ring_step(1)
    w_partner(1)
    moments_to(2)
    w_relay(0, 0)
    ring_step(2)
    w_relay(2, 0)
    w_relay(0, 1)
    w_relay(1, 0)
    moments_to(3)
    ring_step(3)
    w_relay(1, 1)
    w_partner(2)

    moments_to(4)

    side_arrived(7)
    side_arrived(1)
    side_arrived(6)
    side_arrived(2)
    arrived(piece(0, 4, 0), tz_recv.at[4, 0])
    core_send(0, 4, 0)
    arrived(piece(1, 4, 0), tz_recv.at[4, 1])
    side_send(1, 4)
    core_send(1, 4, 0)
    side_arrived(5)
    side_arrived(3)
    for down in (0, 1):
        arrived(*ring_piece(2, 4, down))
    core_send(0, 4, 1)

    first_ones = NDP * n_old // (n_old + n_new)
    grown_at = jnp.maximum(d - first_ones, 0) * 256
    grown_scale = mask_ref[pl.ds(pl.multiple_of(grown_at, 256), 256)].reshape(1, 256)
    is_grown = jnp.where(d >= first_ones, 1.0, 0.0)
    scale = is_grown * grown_scale + (1.0 - is_grown)

    near, far = ((0, 0), (0, 1), (1, 0), (3, 0), (1, 1), (3, 1)), ((2, 0), (2, 1))

    def project(p, blocks, start):
        for h in (0, 1):
            total = None if start else acc[h, p]
            for dx, du in blocks:
                fi = fs(dx, du)
                at = pl.ds(pl.multiple_of(fi * 512, 512), 512)
                part = jnp.dot(
                    T[0 if p < 2 else 1, h * 256 : (h + 1) * 256, at],
                    W[p, at, :],
                    preferred_element_type=F32,
                )
                total = part if total is None else total + part
            acc[h, p] = total

    def pointwise(h):
        gate_value, up_value = acc[h, 0], acc[h, 1]
        sigmoid_gate = jax.nn.sigmoid(gate_value)
        activated = gate_value * sigmoid_gate
        hidden = activated * up_value * scale
        back_hidden = acc[h, 2] * scale
        gate_back = (
            back_hidden * up_value * sigmoid_gate * (1.0 + gate_value * (1.0 - sigmoid_gate))
        )
        up_back = back_hidden * activated
        rounded = hidden.astype(BF)
        H[0, h * 128 : (h + 1) * 128] = rounded[:128]
        H[1, h * 128 : (h + 1) * 128] = rounded[128:]
        cols = slice(h * 256, (h + 1) * 256)
        XT[0:256, cols] = gate_back.T.astype(BF)
        XT[256:512, cols] = up_back.T.astype(BF)
        XT[512:768, cols] = hidden.T.astype(BF)

    for i in (0, 1):
        for k in (0, 1, 7, 2, 6, 3, 5, 4):
            for u in (0, 1):
                if (i, k, u) != (1, 4, 1):
                    arrived(piece(i, k, u, 1), tc_recv.at[k, u, i])
    project(0, near, True)
    w_far(2, 0)
    send(wb(2, 2, 0), wb(2, 2, 0), w_recv.at[2, 7], YP)
    moments_to(5)
    project(1, near, True)
    w_far(0, 0)
    w_far(0, 1)
    project(0, far, False)
    arrived(wb(2, 3, 1), w_recv.at[2, 3])
    arrived(wb(2, 1, 1), w_recv.at[2, 4])
    side_arrived(4)
    arrived(piece(1, 4, 1, 1), tc_recv.at[4, 1, 1])
    project(2, near, True)
    w_far(1, 0)
    w_far(1, 1)
    project(1, far, False)
    arrived(wb(2, 2, 1), w_recv.at[2, 7])
    project(2, far, False)
    pointwise(0)
    pointwise(1)

    def tcols(i, fi):
        return T[i, :, pl.ds(pl.multiple_of(fi * 512, 512), 512)]

    def grad_gu(dx, du):
        G[dx, du, 0:512] = jnp.dot(
            XT[0:512], tcols(0, fs(dx, du)), preferred_element_type=F32
        ).astype(BF)

    def grad_down(dx, du):
        G[dx, du, 512:768] = jnp.dot(
            XT[512:768], tcols(1, fs(dx, du)), preferred_element_type=F32
        ).astype(BF)

    def out_part(v):
        def chunk(j, carry):
            cols = pl.ds(pl.multiple_of(j * 512, 512), 512)
            O[v, :, cols] = lax.dot_general(
                H[v],
                W[2, cols, :],
                (((1,), (1,)), ((), ())),
                preferred_element_type=F32,
            ).astype(BF)
            return carry

        lax.fori_loop(0, 8, chunk, 0)

    def g_first(g, du, lo, n):
        a, b = pl.ds(lo, n // 2), pl.ds(lo + n // 2, n // 2)
        send(G.at[2, du, a, :], R1.at[du, a, :], r1_recv.at[g, 0], XP)
        send(G.at[2, du, b, :], R1.at[du, b, :], r1_recv.at[g, 1], XM)

    def g_second(g, du, lo, n):
        a, b = pl.ds(lo, n // 2), pl.ds(lo + n // 2, n // 2)
        arrived(R1.at[du, a, :], r1_recv.at[g, 0])
        G[1, du, a, :] = (G[1, du, a, :].astype(F32) + R1[du, a, :].astype(F32)).astype(BF)
        w = pl.ds(lo, n)
        send(G.at[1, du, w, :], R2m.at[du, w, :], r2m_recv.at[g], XP)
        arrived(R1.at[du, b, :], r1_recv.at[g, 1])
        G[3, du, b, :] = (G[3, du, b, :].astype(F32) + R1[du, b, :].astype(F32)).astype(BF)
        send(G.at[3, du, w, :], R2p.at[du, w, :], r2p_recv.at[g], XM)

    def g_third(g, du, lo, n):
        w = pl.ds(lo, n)
        arrived(R2m.at[du, w, :], r2m_recv.at[g])
        arrived(R2p.at[du, w, :], r2p_recv.at[g])
        return (
            G[0, du, w, :].astype(F32) + R2m[du, w, :].astype(F32) + R2p[du, w, :].astype(F32)
        )

    grad_gu(2, 1)
    g_first(1, 1, 0, 512)
    grad_gu(2, 0)
    g_first(0, 0, 0, 512)
    out_part(1)
    for h in (0, 1):
        rows = pl.ds(h * 128, 128)
        send(O.at[1, rows, :], RC.at[rows, :], rc_recv.at[h], CP)
    for dx in (2, 1, 3, 0):
        grad_down(dx, 1)
        send(G.at[dx, 1, pl.ds(512, 256), :], RYF.at[dx], ryf_recv.at[dx], YP)
    out_part(0)

    def down_sum(dx):
        arrived(RYF.at[dx], ryf_recv.at[dx])
        G[dx, 0, 512:768, :] = (
            jnp.dot(XT[512:768], tcols(1, fs(dx, 0)), preferred_element_type=F32)
            .astype(BF)
            .astype(F32)
            + RYF[dx].astype(F32)
        ).astype(BF)

    def zrows(k):
        return pl.ds(PLACE[k] * 32, 32)

    def core_sum(h):
        rows = pl.ds(h * 128, 128)
        arrived(RC.at[rows, :], rc_recv.at[h])
        PT[rows, :] = (O[0, rows, :].astype(F32) + RC[rows, :].astype(F32)).astype(BF)

    core_sum(1)
    send(PT.at[zrows(4), left], RZp.at[0, :, left], rzp_recv.at[0], ZP)
    send(PT.at[zrows(4), right], RZm.at[0, :, right], rzm_recv.at[0], ZM)
    moments_to(6)
    grad_gu(1, 1)
    grad_gu(3, 1)
    g_second(1, 1, 0, 512)
    core_sum(0)
    down_sum(2)
    g_first(2, 0, 512, 256)

    def z_step(s):
        whole = pl.ds(0, 4096)
        for k, got, sem, cols, to in (
            (4 - s, RZp, rzp_recv, left if s == 1 else whole, ZP),
            (4 + s, RZm, rzm_recv, right if s == 1 else whole, ZM),
        ):
            arrived(got.at[s - 1, :, cols], sem.at[s - 1])
            PT[zrows(k), cols] = (
                PT[zrows(k), cols].astype(F32) + got[s - 1, :, cols].astype(F32)
            ).astype(BF)
            send(PT.at[zrows(k), :], got.at[s], sem.at[s], to)

    z_step(1)
    moments_to(7)
    grad_gu(1, 0)
    grad_gu(3, 0)
    g_second(0, 0, 0, 512)
    z_step(2)
    moments_to(8)
    down_sum(1)
    down_sum(3)
    g_second(2, 0, 512, 256)
    grad_gu(0, 1)

    RYS[...] = g_third(1, 1, 0, 512).T.astype(BF)
    send(RYS, RY, ry_recv.at[0], YP)
    z_step(3)
    moments_to(9)
    grad_gu(0, 0)
    down_sum(0)

    arrived(RZp.at[3], rzp_recv.at[3])
    arrived(RZm.at[3], rzm_recv.at[3])
    nearby = PT[zrows(0), :].astype(F32) + RZp[3].astype(F32) + RZm[3].astype(F32)
    PT[16:32, :] = nearby[16:].astype(BF)
    send(PT.at[pl.ds(16, 16), :], RYH, ryh_recv.at[0], YN)
    moments_to(10)

    arrived(RYH, ryh_recv.at[0])
    out_ref[...] = (nearby[:16] + RYH[...].astype(F32)).astype(BF)
    both = g_third(0, 0, 0, 512)
    grad_ref[0] = both[:256].T
    grad_ref[1] = both[256:].T
    arrived(RY, ry_recv.at[0])
    for p in (0, 1):
        grad_ref[p] = grad_ref[p] + RY[:, p * 256 : (p + 1) * 256].astype(F32)
    grad_ref[2] = g_third(2, 0, 512, 256).T

    for half, dst in enumerate((fst_hbm, snd_hbm)):
        arrived(dst.at[:, pl.ds(0, 496), :], m_recv.at[half])
    for p in range(3):
        pltpu.make_async_copy(
            stage_w.at[p, pl.ds(0, 31)], stage_w.at[p, pl.ds(0, 31)], a_send.at[p]
        ).wait()
    for half in (0, 1):
        given_all = stage_m.at[pl.ds(0, 31), pl.ds(3 * half, 3)]
        pltpu.make_async_copy(given_all, given_all, m_send.at[half]).wait()
    keep.wait()
    for copy in keep_m:
        copy.wait()
    for copy in sent:
        copy.wait_send()


def local(
    tokens,
    upstream,
    old_master,
    old_first,
    old_second,
    grown_master,
    grown_first,
    grown_second,
    grow_mask,
):
    planes = tuple(
        jnp.transpose(a, (1, 0, 2))
        for a in (old_master, old_first, old_second, grown_master, grown_first, grown_second)
    )
    anyspace = pl.BlockSpec(memory_space=pl.ANY)
    vmem = pl.BlockSpec(memory_space=pltpu.VMEM)
    dma = pltpu.SemaphoreType.DMA
    out, gradients, first, second, master = pl.pallas_call(
        step_kernel,
        out_shape=(
            jax.ShapeDtypeStruct((16, 4096), BF),
            jax.ShapeDtypeStruct((3, 512, 256), F32),
            jax.ShapeDtypeStruct((3, 512, 256), BF),
            jax.ShapeDtypeStruct((3, 512, 256), BF),
            jax.ShapeDtypeStruct((3, 512, 256), BF),
        ),
        in_specs=[anyspace] * 8 + [vmem],
        out_specs=(vmem, vmem, anyspace, anyspace, anyspace),
        scratch_shapes=[
            pltpu.VMEM((3, 16, 8192), F32),
            pltpu.VMEM((6, 16, 8192), F32),
            pltpu.VMEM((3, 32, 16, 256), BF),
            pltpu.VMEM((32, 6, 16, 256), BF),
            pltpu.VMEM((3, 4096, 256), BF),
            pltpu.VMEM((2, 512, 4096), BF),
            pltpu.VMEM((2, 3, 256, 256), F32),
            pltpu.VMEM((2, 256, 256), BF),
            pltpu.VMEM((768, 512), BF),
            pltpu.VMEM((4, 2, 768, 512), BF),
            pltpu.VMEM((2, 768, 512), BF),
            pltpu.VMEM((2, 768, 512), BF),
            pltpu.VMEM((2, 768, 512), BF),
            pltpu.VMEM((512, 512), BF),
            pltpu.VMEM((512, 512), BF),
            pltpu.VMEM((4, 256, 512), BF),
            pltpu.VMEM((2, 256, 4096), BF),
            pltpu.VMEM((256, 4096), BF),
            pltpu.VMEM((256, 4096), BF),
            pltpu.VMEM((4, 32, 4096), BF),
            pltpu.VMEM((4, 32, 4096), BF),
            pltpu.VMEM((16, 4096), BF),
            dma((12,)),
            dma((160,)),
            dma((3,)),
            dma((3,)),
            dma((2,)),
            dma((2,)),
            dma((3,)),
            dma((8, 3)),
            dma((8, 2, 2)),
            dma((8, 2)),
            dma((3, 9)),
            dma((3, 2)),
            dma((3,)),
            dma((3,)),
            dma((1,)),
            dma((4,)),
            dma((2,)),
            dma((4,)),
            dma((4,)),
            dma((1,)),
        ],
        compiler_params=pltpu.CompilerParams(
            collective_id=0, has_side_effects=True, vmem_limit_bytes=64000 * 1024
        ),
        name="grown_step",
    )(tokens, upstream, *planes, grow_mask)
    updated = adam_update(
        master.astype(F32), first.astype(F32), second.astype(F32), gradients
    )
    return (out,) + tuple(jnp.transpose(a, (1, 0, 2)) for a in updated)


def solution(mesh):
    rows = P(("fsdp", "dp"), None)
    stored = P(("fsdp", "dp"), None, None)
    owned = P("fsdp", None, "dp")
    return jax.shard_map(
        local,
        mesh=mesh,
        in_specs=(rows, rows) + (stored,) * 6 + (P(),),
        out_specs=(rows, owned, owned, owned),
        check_vma=False,
    )
```

```python
import functools

import jax
import jax.numpy as jnp
from jax import lax
from jax.experimental import pallas as pl
from jax.experimental.pallas import tpu as pltpu
from jax.sharding import PartitionSpec as P

STEP = 1000

beta_first = 0.9
beta_second = 0.999
adam_epsilon = 1e-08
learn_rate = 0.001
weight_decay = 0.1

BF = jnp.bfloat16
F32 = jnp.float32
MESH = pl.DeviceIdType.MESH

NX, NZ, NDP = 4, 8, 32
MOMENTS = (
    (0, 0), (0, 0), (0, 0), (0, 0), (15, 0), (15, 4), (15, 7), (15, 10), (15, 13), (15, 16), (15, 16),
)
Q = 0
XF, YF = 512 + Q, 256 - Q
PLACE = {k: i for i, k in enumerate((0, 1, 7, 2, 6, 3, 5, 4))}


def adam_update(master, first_moment, second_moment, gradients):
    new_first = beta_first * first_moment + (1.0 - beta_first) * gradients
    new_second = beta_second * second_moment + (1.0 - beta_second) * gradients * gradients
    first_hat = new_first / (1.0 - beta_first**STEP)
    second_hat = new_second / (1.0 - beta_second**STEP)
    new_master = master - learn_rate * (
        first_hat / (jnp.sqrt(second_hat) + adam_epsilon) + weight_decay * master
    )
    return (new_master, new_first, new_second)


def step_kernel(
    tok_hbm,
    ups_hbm,
    om_hbm,
    of_hbm,
    os_hbm,
    gm_hbm,
    gf_hbm,
    gs_hbm,
    mask_ref,
    out_ref,
    grad_ref,
    fst_hbm,
    snd_hbm,
    mas_hbm,
    mf,
    momf,
    stage_w,
    stage_m,
    W,
    T,
    acc,
    H,
    XT,
    G,
    R1,
    R2m,
    R2p,
    RY,
    RYS,
    RYF,
    O,
    RC,
    PT,
    RZp,
    RZm,
    RYH,
    load_sems,
    send_sems,
    a_send,
    a_recv,
    m_send,
    m_recv,
    own_sems,
    tz_recv,
    tc_recv,
    ty_recv,
    w_recv,
    r1_recv,
    r2m_recv,
    r2p_recv,
    ry_recv,
    ryf_recv,
    rc_recv,
    rzp_recv,
    rzm_recv,
    ryh_recv,
):
    f = lax.axis_index("fsdp")
    d = lax.axis_index("dp")
    x, yl = lax.div(f, 2), lax.rem(f, 2)
    yh, z, c = lax.div(d, 16), lax.rem(lax.div(d, 2), NZ), lax.rem(d, 2)

    def fs(dx, du):
        ylu = yl if du == 0 else 1 - yl
        return lax.rem(x + dx, NX) * 2 + ylu

    def dpi(dz, du, dv):
        yhu = yh if du == 0 else 1 - yh
        cv = c if dv == 0 else 1 - c
        return (yhu * NZ + lax.rem(z + dz, NZ)) * 2 + cv

    XP, XM, YP = {"fsdp": fs(1, 0)}, {"fsdp": fs(3, 0)}, {"fsdp": fs(0, 1)}
    ZP, ZM = {"dp": dpi(1, 0, 0)}, {"dp": dpi(7, 0, 0)}
    CP = {"dp": dpi(0, 0, 1)}
    YN = {"dp": dpi(0, 1, 0), "fsdp": fs(0, 1)}

    sent = []

    def send(src, dst, rsem, dev):
        copy = pltpu.make_async_remote_copy(
            src_ref=src,
            dst_ref=dst,
            send_sem=send_sems.at[len(sent)],
            recv_sem=rsem,
            device_id=dev,
            device_id_type=MESH,
        )
        copy.start()
        sent.append(copy)

    def arrived(dst, rsem):
        pltpu.make_async_copy(dst, dst, rsem).wait()

    loads = []

    def load(src, dst):
        copy = pltpu.make_async_copy(src, dst, load_sems.at[len(loads)])
        copy.start()
        loads.append(copy)
        return copy

    n_old = om_hbm.shape[2]
    n_new = gm_hbm.shape[2]
    load_w = [
        (
            load(om_hbm.at[p], mf.at[p, :, pl.ds(0, n_old)]),
            load(gm_hbm.at[p], mf.at[p, :, pl.ds(n_old, n_new)]),
        )
        for p in range(3)
    ]

    def row(k, u, v):
        at = PLACE[k]
        return (at // 4) * 256 + v * 128 + ((at % 4) * 2 + u) * 16

    def blk(k, u, v):
        return T.at[:, pl.ds(row(k, u, v), 16), :]

    load_t = [
        load(tok_hbm, T.at[0, pl.ds(row(0, 0, 0), 16), :]),
        load(ups_hbm, T.at[1, pl.ds(row(0, 0, 0), 16), :]),
    ]
    load_m = [
        load(of_hbm, momf.at[pl.ds(0, 3), :, pl.ds(0, n_old)]),
        load(gf_hbm, momf.at[pl.ds(0, 3), :, pl.ds(n_old, n_new)]),
        load(os_hbm, momf.at[pl.ds(3, 3), :, pl.ds(0, n_old)]),
        load(gs_hbm, momf.at[pl.ds(3, 3), :, pl.ds(n_old, n_new)]),
    ]

    def other(i):
        half = lax.div(i + 1, 2)
        turn = 1 - 2 * lax.rem(i + 1, 2)
        return lax.rem(d + NDP + turn * half, NDP)

    barrier = pltpu.get_barrier_semaphore()

    def greet(i, carry):
        pl.semaphore_signal(
            barrier, inc=1, device_id={"dp": other(i)}, device_id_type=MESH
        )
        return carry

    lax.fori_loop(1, NDP, greet, 0)
    for dev in (XP, XM, YP, YN):
        pl.semaphore_signal(barrier, inc=1, device_id=dev, device_id_type=MESH)

    def wrow(fi, lo, n):
        return pl.ds(pl.multiple_of(fi * 512 + lo, 16), n)

    def mine16(lo):
        return pl.ds(pl.multiple_of(lo + d * 16, 16), 16)

    for p in range(3):
        for copy in load_w[p]:
            copy.wait()
        for j in range(NDP):
            stage_w[p, j] = mf[p, :, j * 256 : (j + 1) * 256].astype(BF)
        W[p, mine16(f * 512), :] = stage_w[p, d]
        if p == 0:
            pl.semaphore_wait(barrier, NDP - 1 + 4)

        def give(i, carry, p=p):
            to = other(i)
            pltpu.make_async_remote_copy(
                src_ref=stage_w.at[p, to],
                dst_ref=W.at[p, mine16(f * 512), :],
                send_sem=a_send.at[p],
                recv_sem=a_recv.at[p],
                device_id={"dp": to},
                device_id_type=MESH,
            ).start()
            return carry

        lax.fori_loop(1, NDP, give, 0)

    def piece(i, k, u, v=0):
        return T.at[i, pl.ds(row(k, u, v), 16), :]

    def core_send(i, k, u):
        send(piece(i, k, u), piece(i, k, u, 1), tc_recv.at[k, u, i], CP)

    def side_send(i, k):
        send(piece(i, k, 0), piece(i, k, 1), ty_recv.at[k, i], YN)

    left, right = pl.ds(0, 2048), pl.ds(2048, 2048)
    streams = ((0, 0), (1, 0), (0, 1))

    def ring_piece(j, k, down):
        i, u = streams[j]
        if k != 4:
            return piece(i, k, u), tz_recv.at[k, j]
        if j == 2:
            half = right if down else left
            return T.at[i, pl.ds(row(k, u, 0), 16), half], tz_recv.at[0 if down else 4, j]
        return (piece(i, k, u), tz_recv.at[4, j]) if j == down else (None, None)

    def ring_send(j, s, down):
        a, b = (s, s + 1) if down else ((8 - s) % 8, 7 - s)
        dst, sem = ring_piece(j, b, down)
        if dst is None:
            return
        i, u = streams[j]
        src = piece(i, a, u)
        if b == 4 and j == 2:
            src = T.at[i, pl.ds(row(a, u, 0), 16), right if down else left]
        send(src, dst, sem, ZM if down else ZP)

    def ring_step(s):
        for j, (i, u) in enumerate(streams):
            for down in (0, 1):
                k = s if down else (8 - s) % 8
                arrived(piece(i, k, u), tz_recv.at[k, j])
                ring_send(j, s, down)
            for k in ((8 - s) % 8, s):
                if j == 1:
                    side_send(1, k)
                core_send(i, k, u)

    def side_arrived(k):
        arrived(piece(1, k, 1), ty_recv.at[k, 1])
        core_send(1, k, 1)

    for copy in load_t:
        copy.wait()
    for i in (0, 1):
        side_send(i, 0)
        for down in (0, 1):
            ring_send(i, 0, down)
        core_send(i, 0, 0)

    for copy in load_m:
        copy.wait()

    def stage_moments(q, carry):
        for j in range(NDP):
            stage_m[j, q] = momf[q, :, j * 256 : (j + 1) * 256].astype(BF)
        return carry

    lax.fori_loop(0, 6, stage_moments, 0)

    def wb(p, dx, du, lo=0, n=512):
        return W.at[p, wrow(fs(dx, du), lo, n), :]

    def w_own(p):
        arrived(W.at[p, wrow(f, 0, 496), :], a_recv.at[p])
        send(wb(p, 0, 0), wb(p, 0, 0), w_recv.at[p, 2], YP)
        send(wb(p, 0, 0), wb(p, 0, 0), w_recv.at[p, 0], XP)
        send(wb(p, 0, 0), wb(p, 0, 0), w_recv.at[p, 1], XM)

    def w_partner(p):
        arrived(wb(p, 0, 1), w_recv.at[p, 2])
        if p < 2:
            send(wb(p, 0, 1), wb(p, 0, 1), w_recv.at[p, 3], XP)
            send(wb(p, 0, 1), wb(p, 0, 1), w_recv.at[p, 4], XM)

    def w_relay(p, du):
        arrived(wb(p, 3, du), w_recv.at[p, 3 * du])
        send(wb(p, 3, du, 0, 256), wb(p, 3, du, 0, 256), w_recv.at[p, 5 + 2 * du], XP)
        if p == 2:
            send(wb(p, 3, 0), wb(p, 3, 0), w_recv.at[p, 3], YP)
        arrived(wb(p, 1, du), w_recv.at[p, 3 * du + 1])
        send(wb(p, 1, du, 256, 256), wb(p, 1, du, 256, 256), w_recv.at[p, 6 + 2 * du], XM)
        if p == 2:
            send(wb(p, 1, 0), wb(p, 1, 0), w_recv.at[p, 4], YP)

    def w_far(p, du):
        arrived(wb(p, 2, du, 0, 256), w_recv.at[p, 5 + 2 * du])
        arrived(wb(p, 2, du, 256, 256), w_recv.at[p, 6 + 2 * du])

    def give_moments(i, carry):
        r = lax.rem(i, 16)
        turn = (1 - 2 * lax.rem(r + 1, 2)) * lax.div(r + 1, 2)
        there = yh + lax.div(i, 16) * (1 - 2 * yh)
        to = there * 16 + lax.rem(lax.rem(d, 16) + 16 + turn, 16)
        for half, dst in enumerate((fst_hbm, snd_hbm)):
            pltpu.make_async_remote_copy(
                src_ref=stage_m.at[to, pl.ds(3 * half, 3)],
                dst_ref=dst.at[:, mine16(0), :],
                send_sem=m_send.at[half],
                recv_sem=m_recv.at[half],
                device_id={"dp": to},
                device_id_type=MESH,
            ).start()
        return carry

    given = [1, 16]

    def moments_to(point):
        for side, n in enumerate(MOMENTS[point]):
            n += 1 + 15 * side
            if n > given[side]:
                lax.fori_loop(given[side], n, give_moments, 0)
                given[side] = n

    keep_m = [
        pltpu.make_async_copy(
            stage_m.at[d, pl.ds(3 * half, 3)], dst.at[:, mine16(0), :], own_sems.at[1 + half]
        )
        for half, dst in enumerate((fst_hbm, snd_hbm))
    ]
    for copy in keep_m:
        copy.start()

    w_own(0)
    moments_to(0)
    arrived(piece(0, 0, 1), ty_recv.at[0, 0])
    for down in (0, 1):
        ring_send(2, 0, down)
    core_send(0, 0, 1)
    side_arrived(0)
    w_own(1)
    w_partner(0)
    ring_step(1)
    w_own(2)
    keep = pltpu.make_async_copy(W.at[:, wrow(f, 0, 512), :], mas_hbm, own_sems.at[0])
    keep.start()
    moments_to(1)
    w_partner(1)
    moments_to(2)
    w_relay(0, 0)
    ring_step(2)
    w_relay(2, 0)
    w_relay(0, 1)
    w_relay(1, 0)
    moments_to(3)
    ring_step(3)
    w_relay(1, 1)
    w_partner(2)

    moments_to(4)

    side_arrived(7)
    side_arrived(1)
    side_arrived(6)
    side_arrived(2)
    arrived(piece(0, 4, 0), tz_recv.at[4, 0])
    core_send(0, 4, 0)
    arrived(piece(1, 4, 0), tz_recv.at[4, 1])
    side_send(1, 4)
    core_send(1, 4, 0)
    side_arrived(5)
    side_arrived(3)
    for down in (0, 1):
        arrived(*ring_piece(2, 4, down))
    core_send(0, 4, 1)

    first_ones = NDP * n_old // (n_old + n_new)
    grown_at = jnp.maximum(d - first_ones, 0) * 256
    grown_scale = mask_ref[pl.ds(pl.multiple_of(grown_at, 256), 256)].reshape(1, 256)
    is_grown = jnp.where(d >= first_ones, 1.0, 0.0)
    scale = is_grown * grown_scale + (1.0 - is_grown)

    near, far = ((0, 0), (0, 1), (1, 0), (3, 0), (1, 1), (3, 1)), ((2, 0), (2, 1))

    def project(p, blocks, start):
        for h in (0, 1):
            total = None if start else acc[h, p]
            for dx, du in blocks:
                fi = fs(dx, du)
                at = pl.ds(pl.multiple_of(fi * 512, 512), 512)
                part = jnp.dot(
                    T[0 if p < 2 else 1, h * 256 : (h + 1) * 256, at],
                    W[p, at, :],
                    preferred_element_type=F32,
                )
                total = part if total is None else total + part
            acc[h, p] = total

    def pointwise(h):
        gate_value, up_value = acc[h, 0], acc[h, 1]
        sigmoid_gate = jax.nn.sigmoid(gate_value)
        activated = gate_value * sigmoid_gate
        hidden = activated * up_value * scale
        back_hidden = acc[h, 2] * scale
        gate_back = (
            back_hidden * up_value * sigmoid_gate * (1.0 + gate_value * (1.0 - sigmoid_gate))
        )
        up_back = back_hidden * activated
        rounded = hidden.astype(BF)
        H[0, h * 128 : (h + 1) * 128] = rounded[:128]
        H[1, h * 128 : (h + 1) * 128] = rounded[128:]
        cols = slice(h * 256, (h + 1) * 256)
        XT[0:256, cols] = gate_back.T.astype(BF)
        XT[256:512, cols] = up_back.T.astype(BF)
        XT[512:768, cols] = hidden.T.astype(BF)

    for i in (0, 1):
        for k in (0, 1, 7, 2, 6, 3, 5, 4):
            for u in (0, 1):
                if (i, k, u) != (1, 4, 1):
                    arrived(piece(i, k, u, 1), tc_recv.at[k, u, i])
    project(0, near, True)
    w_far(2, 0)
    send(wb(2, 2, 0), wb(2, 2, 0), w_recv.at[2, 7], YP)
    moments_to(5)
    project(1, near, True)
    w_far(0, 0)
    w_far(0, 1)
    project(0, far, False)
    arrived(wb(2, 3, 1), w_recv.at[2, 3])
    arrived(wb(2, 1, 1), w_recv.at[2, 4])
    side_arrived(4)
    arrived(piece(1, 4, 1, 1), tc_recv.at[4, 1, 1])
    project(2, near, True)
    w_far(1, 0)
    w_far(1, 1)
    project(1, far, False)
    arrived(wb(2, 2, 1), w_recv.at[2, 7])
    project(2, far, False)
    pointwise(0)
    pointwise(1)

    def tcols(i, fi):
        return T[i, :, pl.ds(pl.multiple_of(fi * 512, 512), 512)]

    def grad_gu(dx, du):
        G[dx, du, 0:512] = jnp.dot(
            XT[0:512], tcols(0, fs(dx, du)), preferred_element_type=F32
        ).astype(BF)
        if Q:
            G[dx, du, 512:XF] = jnp.dot(
                XT[512:XF], tcols(1, fs(dx, du)), preferred_element_type=F32
            ).astype(BF)

    def grad_down(dx, du):
        G[dx, du, XF:768] = jnp.dot(
            XT[XF:768], tcols(1, fs(dx, du)), preferred_element_type=F32
        ).astype(BF)

    def out_part(v):
        def chunk(j, carry):
            cols = pl.ds(pl.multiple_of(j * 512, 512), 512)
            O[v, :, cols] = lax.dot_general(
                H[v],
                W[2, cols, :],
                (((1,), (1,)), ((), ())),
                preferred_element_type=F32,
            ).astype(BF)
            return carry

        lax.fori_loop(0, 8, chunk, 0)

    def g_first(g, du, lo, n):
        a, b = pl.ds(lo, n // 2), pl.ds(lo + n // 2, n // 2)
        send(G.at[2, du, a, :], R1.at[du, a, :], r1_recv.at[g, 0], XP)
        send(G.at[2, du, b, :], R1.at[du, b, :], r1_recv.at[g, 1], XM)

    def g_second(g, du, lo, n):
        a, b = pl.ds(lo, n // 2), pl.ds(lo + n // 2, n // 2)
        arrived(R1.at[du, a, :], r1_recv.at[g, 0])
        G[1, du, a, :] = (G[1, du, a, :].astype(F32) + R1[du, a, :].astype(F32)).astype(BF)
        w = pl.ds(lo, n)
        send(G.at[1, du, w, :], R2m.at[du, w, :], r2m_recv.at[g], XP)
        arrived(R1.at[du, b, :], r1_recv.at[g, 1])
        G[3, du, b, :] = (G[3, du, b, :].astype(F32) + R1[du, b, :].astype(F32)).astype(BF)
        send(G.at[3, du, w, :], R2p.at[du, w, :], r2p_recv.at[g], XM)

    def g_third(g, du, lo, n):
        w = pl.ds(lo, n)
        arrived(R2m.at[du, w, :], r2m_recv.at[g])
        arrived(R2p.at[du, w, :], r2p_recv.at[g])
        return (
            G[0, du, w, :].astype(F32) + R2m[du, w, :].astype(F32) + R2p[du, w, :].astype(F32)
        )

    grad_gu(2, 1)
    g_first(1, 1, 0, XF)
    for dx in (2, 1, 3, 0):
        grad_down(dx, 1)
        send(G.at[dx, 1, pl.ds(XF, YF), :], RYF.at[dx], ryf_recv.at[dx], YP)
    grad_gu(2, 0)
    g_first(0, 0, 0, XF)
    out_part(1)
    for h in (0, 1):
        rows = pl.ds(h * 128, 128)
        send(O.at[1, rows, :], RC.at[rows, :], rc_recv.at[h], CP)
    out_part(0)

    def down_sum(dx):
        arrived(RYF.at[dx], ryf_recv.at[dx])
        G[dx, 0, XF:768, :] = (
            jnp.dot(XT[XF:768], tcols(1, fs(dx, 0)), preferred_element_type=F32)
            .astype(BF)
            .astype(F32)
            + RYF[dx].astype(F32)
        ).astype(BF)

    def zrows(k):
        return pl.ds(PLACE[k] * 32, 32)

    def core_sum(h):
        rows = pl.ds(h * 128, 128)
        arrived(RC.at[rows, :], rc_recv.at[h])
        PT[rows, :] = (O[0, rows, :].astype(F32) + RC[rows, :].astype(F32)).astype(BF)

    core_sum(1)
    send(PT.at[zrows(4), left], RZp.at[0, :, left], rzp_recv.at[0], ZP)
    send(PT.at[zrows(4), right], RZm.at[0, :, right], rzm_recv.at[0], ZM)
    moments_to(6)
    grad_gu(1, 1)
    grad_gu(3, 1)
    g_second(1, 1, 0, XF)
    core_sum(0)
    down_sum(2)
    g_first(2, 0, XF, YF)

    def z_step(s):
        whole = pl.ds(0, 4096)
        for k, got, sem, cols, to in (
            (4 - s, RZp, rzp_recv, left if s == 1 else whole, ZP),
            (4 + s, RZm, rzm_recv, right if s == 1 else whole, ZM),
        ):
            arrived(got.at[s - 1, :, cols], sem.at[s - 1])
            PT[zrows(k), cols] = (
                PT[zrows(k), cols].astype(F32) + got[s - 1, :, cols].astype(F32)
            ).astype(BF)
            send(PT.at[zrows(k), :], got.at[s], sem.at[s], to)

    z_step(1)
    moments_to(7)
    grad_gu(1, 0)
    grad_gu(3, 0)
    g_second(0, 0, 0, XF)
    z_step(2)
    moments_to(8)
    down_sum(1)
    down_sum(3)
    g_second(2, 0, XF, YF)
    grad_gu(0, 1)

    RYS[...] = g_third(1, 1, 0, XF).T.astype(BF)
    send(RYS, RY, ry_recv.at[0], YP)
    z_step(3)
    moments_to(9)
    grad_gu(0, 0)
    down_sum(0)

    arrived(RZp.at[3], rzp_recv.at[3])
    arrived(RZm.at[3], rzm_recv.at[3])
    nearby = PT[zrows(0), :].astype(F32) + RZp[3].astype(F32) + RZm[3].astype(F32)
    PT[16:32, :] = nearby[16:].astype(BF)
    send(PT.at[pl.ds(16, 16), :], RYH, ryh_recv.at[0], YN)
    moments_to(10)

    arrived(RYH, ryh_recv.at[0])
    out_ref[...] = (nearby[:16] + RYH[...].astype(F32)).astype(BF)
    both = g_third(0, 0, 0, XF)
    grad_ref[0] = both[:256].T
    grad_ref[1] = both[256:512].T
    if Q:
        grad_ref[2, :, 0:Q] = both[512:].T
    arrived(RY, ry_recv.at[0])
    for p in (0, 1):
        grad_ref[p] = grad_ref[p] + RY[:, p * 256 : (p + 1) * 256].astype(F32)
    if Q:
        grad_ref[2, :, 0:Q] = grad_ref[2, :, 0:Q] + RY[:, 512:].astype(F32)
    grad_ref[2, :, Q:] = g_third(2, 0, XF, YF).T

    for half, dst in enumerate((fst_hbm, snd_hbm)):
        arrived(dst.at[:, pl.ds(0, 496), :], m_recv.at[half])
    for p in range(3):
        pltpu.make_async_copy(
            stage_w.at[p, pl.ds(0, 31)], stage_w.at[p, pl.ds(0, 31)], a_send.at[p]
        ).wait()
    for half in (0, 1):
        given_all = stage_m.at[pl.ds(0, 31), pl.ds(3 * half, 3)]
        pltpu.make_async_copy(given_all, given_all, m_send.at[half]).wait()
    keep.wait()
    for copy in keep_m:
        copy.wait()
    for copy in sent:
        copy.wait_send()


def local(
    tokens,
    upstream,
    old_master,
    old_first,
    old_second,
    grown_master,
    grown_first,
    grown_second,
    grow_mask,
):
    planes = tuple(
        jnp.transpose(a, (1, 0, 2))
        for a in (old_master, old_first, old_second, grown_master, grown_first, grown_second)
    )
    anyspace = pl.BlockSpec(memory_space=pl.ANY)
    vmem = pl.BlockSpec(memory_space=pltpu.VMEM)
    dma = pltpu.SemaphoreType.DMA
    out, gradients, first, second, master = pl.pallas_call(
        step_kernel,
        out_shape=(
            jax.ShapeDtypeStruct((16, 4096), BF),
            jax.ShapeDtypeStruct((3, 512, 256), F32),
            jax.ShapeDtypeStruct((3, 512, 256), BF),
            jax.ShapeDtypeStruct((3, 512, 256), BF),
            jax.ShapeDtypeStruct((3, 512, 256), BF),
        ),
        in_specs=[anyspace] * 8 + [vmem],
        out_specs=(vmem, vmem, anyspace, anyspace, anyspace),
        scratch_shapes=[
            pltpu.VMEM((3, 16, 8192), F32),
            pltpu.VMEM((6, 16, 8192), F32),
            pltpu.VMEM((3, 32, 16, 256), BF),
            pltpu.VMEM((32, 6, 16, 256), BF),
            pltpu.VMEM((3, 4096, 256), BF),
            pltpu.VMEM((2, 512, 4096), BF),
            pltpu.VMEM((2, 3, 256, 256), F32),
            pltpu.VMEM((2, 256, 256), BF),
            pltpu.VMEM((768, 512), BF),
            pltpu.VMEM((4, 2, 768, 512), BF),
            pltpu.VMEM((2, 768, 512), BF),
            pltpu.VMEM((2, 768, 512), BF),
            pltpu.VMEM((2, 768, 512), BF),
            pltpu.VMEM((512, XF), BF),
            pltpu.VMEM((512, XF), BF),
            pltpu.VMEM((4, YF, 512), BF),
            pltpu.VMEM((2, 256, 4096), BF),
            pltpu.VMEM((256, 4096), BF),
            pltpu.VMEM((256, 4096), BF),
            pltpu.VMEM((4, 32, 4096), BF),
            pltpu.VMEM((4, 32, 4096), BF),
            pltpu.VMEM((16, 4096), BF),
            dma((12,)),
            dma((160,)),
            dma((3,)),
            dma((3,)),
            dma((2,)),
            dma((2,)),
            dma((3,)),
            dma((8, 3)),
            dma((8, 2, 2)),
            dma((8, 2)),
            dma((3, 9)),
            dma((3, 2)),
            dma((3,)),
            dma((3,)),
            dma((1,)),
            dma((4,)),
            dma((2,)),
            dma((4,)),
            dma((4,)),
            dma((1,)),
        ],
        compiler_params=pltpu.CompilerParams(
            collective_id=0, has_side_effects=True, vmem_limit_bytes=64000 * 1024
        ),
        name="grown_step",
    )(tokens, upstream, *planes, grow_mask)
    updated = adam_update(
        master.astype(F32), first.astype(F32), second.astype(F32), gradients
    )
    return (out,) + tuple(jnp.transpose(a, (1, 0, 2)) for a in updated)


def solution(mesh):
    rows = P(("fsdp", "dp"), None)
    stored = P(("fsdp", "dp"), None, None)
    owned = P("fsdp", None, "dp")
    return jax.shard_map(
        local,
        mesh=mesh,
        in_specs=(rows, rows) + (stored,) * 6 + (P(),),
        out_specs=(rows, owned, owned, owned),
        check_vma=False,
    )
```
